256 devices in a mesh: va: 8 (over x, y_lo), vb: 8 (over z), aux: 4 (over y_hi, core).
Axes of the slice: x: 4, y: 4 (y_hi: 2, y_lo: 2; y = y_hi * 2 + y_lo), z: 8, core: 2. Of those that a mesh axis runs over, the one named last changes fastest.
Arguments:
- factors: float32 [1024, 8, 2048], P(None, None, 'va'), may hold values from -0.046875 to 0.046875
- domains: int32 [8, 16, 8], replicated, may hold values from 0 to 1, as said below
- occ_energy: float32 [8], replicated, may hold values from -3 to -0.5
- vir_energy: float32 [2048], replicated, may hold values from 0.5 to 3
Outputs:
- amplitudes: float32 [8, 2048, 8, 2048], P(None, 'va', 'aux', 'vb')
The draws below stay inside these ranges and needn't reach their ends.
Inputs may be any that keep to these rules, and one draw needn't show every extreme that they name: `domains`: for every occupied orbital and every block of 128 virtuals, exactly 6 of the 8 fitting blocks are 1.
All inputs are finite; a program needn't handle non-finite values.
Results may differ from the reference program's by a relative error of at most 0.000096.
Values sent between devices are 32-bit elements; how exact they have to be, the bound alone decides.
A program may use at most 128 MiB of HBM per device.

```python
import math
import jax
import jax.numpy as jnp
from jax import lax

O = 8
V = 2048
NAUX = 1024
BLK = 128
PRESENT = 6
NVB = 16
NPB = 8


def draw_domains(key, part):
    scores = jax.random.randint(key, (O, NVB, NPB), 0, 1 << 20) * NPB + jnp.arange(NPB, dtype=jnp.int32)
    picks = lax.top_k(scores, PRESENT)[1]
    hits = (picks[..., None] == jnp.arange(NPB, dtype=jnp.int32)).astype(jnp.int32)
    return jnp.sum(hits, axis=-2).astype(jnp.int32)


def levels(key, extent, split, smallest, top_value):
    gain, own = 1.0, jax.random.fold_in(key, 6)
    for position, blocks in split:
        draws = jnp.exp(jax.random.uniform(jax.random.fold_in(own, position), (blocks,), jnp.float32, smallest / len(split), top_value / len(split)))
        gain = gain * jnp.repeat(draws, extent[position] // blocks).reshape([-1 if axis == position else 1 for axis in range(len(extent))])
    return gain


def scatter_about(own_key, extent, deviation, bound, shards=(), kind=jnp.bfloat16):
    entries = jax.random.normal(own_key, extent, jnp.float32) * deviation
    if len(shards) > 0:
        entries = levels(own_key, extent, shards, -0.22, 0.18) * entries
    return jnp.clip(entries, min=-bound, max=bound).astype(kind)


def setup_inputs(seed: int = 0) -> dict:
    key_of = jax.random.split(jax.random.key(seed), 5)
    return {
        "factors": scatter_about(key_of[0], (NAUX, O, V), (O * V) ** -0.5, 0.046875, ((2, 8),), jnp.float32),
        "domains": draw_domains(jax.random.fold_in(key_of[4], 71), 0),
        "occ_energy": jnp.clip(jax.random.uniform(key_of[2], (O,), jnp.float32, -3.0, -0.5), -3.0, -0.5),
        "vir_energy": jnp.clip(jax.random.uniform(key_of[3], (V,), jnp.float32, 0.5, 3.0), 0.5, 3.0),
    }


highest = lax.Precision.HIGHEST

def spread_mask(domains):
    expanded = jnp.transpose(domains, (2, 0, 1)).astype(jnp.float32)
    fit_blocks, orbitals, vir_blocks = expanded.shape
    expanded = jnp.broadcast_to(expanded[:, None, :, :, None], (fit_blocks, BLK, orbitals, vir_blocks, BLK))
    return expanded.reshape(fit_blocks * BLK, orbitals, vir_blocks * BLK)

def contract_first(left, right):
    return lax.dot_general(left, right, (((0,), (0,)), ((), ())), precision=highest, preferred_element_type=jnp.float32)

def reference(factors, domains, occ_energy, vir_energy):
    weights = spread_mask(domains)
    masked = factors * weights
    flattened = masked.reshape(NAUX, O * V)
    weight_flat = weights.reshape(NAUX, O * V)
    vir_pair = vir_energy[:, None, None] + vir_energy[None, None, :] - occ_energy[None, :, None]

    def block_denominator(index):
        return (vir_pair - occ_energy[index]).reshape(V, O * V)

    def first_block(index):
        rows = lax.dynamic_slice_in_dim(flattened, index * V, V, 1)
        direct_rows = contract_first(rows, flattened)
        first_rows = -direct_rows / block_denominator(index)
        dressed_rows = lax.dot_general(flattened, first_rows, (((1,), (1,)), ((), ())), precision=highest, preferred_element_type=jnp.float32)
        return (dressed_rows, direct_rows)
    indices = jnp.arange(O, dtype=jnp.int32)
    dressed_blocks, direct_blocks = lax.map(first_block, indices)
    dressed = jnp.transpose(dressed_blocks, (1, 0, 2)).reshape(NAUX, O * V) * weight_flat
    summed_factors = flattened + dressed

    def second_block(carried):
        index, direct_rows = carried
        rows_sum = lax.dynamic_slice_in_dim(summed_factors, index * V, V, 1)
        rows_dressed = lax.dynamic_slice_in_dim(dressed, index * V, V, 1)
        cross_rows = 2.0 * contract_first(rows_dressed, summed_factors)
        mirror_rows = 2.0 * contract_first(rows_sum, dressed)
        second_rows = -(direct_rows + cross_rows + mirror_rows) / block_denominator(index)
        return (second_rows * (8.0 * O * V / math.sqrt(NAUX))).reshape(V, O, V)
    return lax.map(second_block, (indices, direct_blocks))
```

```python
import functools
import math

import jax
import jax.numpy as jnp
from jax import lax
from jax.experimental import pallas as pl
from jax.experimental.pallas import tpu as pltpu
from jax.sharding import PartitionSpec as P

O = 8
V = 2048
NAUX = 1024
BLK = 128
PRESENT = 6
NPB = 8
NVB = 16
TILE = 256
ROWS = O * TILE
PAIR = 2 * TILE
PACK = PRESENT * BLK
SLICE = PAIR // 8
HALF = SLICE // 2
CHUNKS = 8
LAG = 2
RING_LAG = 3
SCALE = 8.0 * O * V / math.sqrt(NAUX)
MESH = pl.DeviceIdType.MESH
F32 = jnp.float32
BF16 = jnp.bfloat16
VMEM_LIMIT = 60 * 1024 * 1024

TREES = (
    {0: (1,), 1: (2, 5), 2: (3, 6), 5: (4,), 6: (7,)},
    {0: (3,), 3: (2, 7), 2: (1,), 7: (4, 6), 6: (5,)},
    {0: (4,), 4: (5, 7), 5: (6, 1), 6: (2,), 7: (3,)},
)


def split(value):
    high = value.astype(BF16)
    return high, (value - high.astype(F32)).astype(BF16)


def dot_nt(left, right):
    return lax.dot_general(left, right, (((1,), (1,)), ((), ())), preferred_element_type=F32)


def dot_nn(left, right):
    return lax.dot_general(left, right, (((1,), (0,)), ((), ())), preferred_element_type=F32)


def unpack(table, slots, packed, block, high, low, row, scale=None):
    for p in range(NPB):
        entry = block * NPB + p
        slot = jnp.minimum(slots[entry], PRESENT - 1)
        keep = table[entry].astype(F32)
        value = packed(pl.ds(pl.multiple_of(slot * BLK, BLK), BLK)) * keep
        h, l = split(value)
        high[row : row + BLK, p * BLK : (p + 1) * BLK] = h
        low[row : row + BLK, p * BLK : (p + 1) * BLK] = l


def prep_kernel(table, slots, first, second, high, low, packed):
    p = pl.program_id(0)
    va = lax.axis_index("va")
    for i in range(O):
        for half, factors in enumerate((first, second)):
            entry = (i * NVB + va * 2 + half) * NPB + p
            keep = table[entry]
            block = factors[pl.ds(i, BLK, stride=O), :].T * keep.astype(F32)
            row = i * TILE + half * BLK
            h, l = split(block)
            high[row : row + BLK, :] = h
            low[row : row + BLK, :] = l
            slot = jnp.minimum(slots[entry], PRESENT - 1)

            @pl.when(keep > 0)
            def _():
                packed[row : row + BLK, pl.ds(pl.multiple_of(slot * BLK, BLK), BLK)] = block


def spread_kernel(packed, out, send, recv, local):
    va, vb, aux = lax.axis_index("va"), lax.axis_index("vb"), lax.axis_index("aux")
    barrier = pltpu.get_barrier_semaphore()
    for k in range(1, 8):
        pl.semaphore_signal(barrier, 1, device_id={"va": (va + k) % 8}, device_id_type=MESH)
    pl.semaphore_wait(barrier, 7)
    root_x, root_y = vb // 2, vb % 2
    node = (va // 2 - root_x + 4) % 4 + 4 * ((va % 2 + root_y) % 2)

    def lookup(values):
        found = jnp.int32(values[0])
        for n in range(1, 8):
            found = jnp.where(node == n, jnp.int32(values[n]), found)
        return found

    skews, childs = [], []
    for tree in TREES:
        depth = {0: 0}
        todo = [0]
        for n in todo:
            for member in tree.get(n, ()):
                depth[member] = depth[n] + 1
                todo.append(member)
        skews.append(lookup([LAG * depth[n] for n in range(8)]))
        childs.append([lookup([(*tree.get(n, ()), -1, -1)[k] for n in range(8)]) for k in range(2)])

    def copy(tree, chunk, child, member):
        ref = out.at[pl.ds(pl.multiple_of(chunk * SLICE, SLICE), SLICE), pl.ds(tree * 256, 256)]
        place = ((root_x + member % 4) % 4) * 2 + (root_y + member // 4) % 2
        return pltpu.make_async_remote_copy(
            ref, ref, send.at[tree, chunk, child], recv.at[tree, chunk], device_id={"va": place}, device_id_type=MESH
        )

    @pl.when(node == 0)
    def _():
        own = pltpu.make_async_copy(packed.at[pl.ds(pl.multiple_of(aux * PAIR, PAIR), PAIR), :], out, local)
        own.start()
        own.wait()

    def step(t, carry):
        for tree in range(3):
            chunk = t - skews[tree]

            @pl.when((chunk >= 0) & (chunk < CHUNKS))
            def _():
                @pl.when(node != 0)
                def _():
                    copy(tree, chunk, 0, 0).wait_recv()

                for k in range(2):
                    member = childs[tree][k]

                    @pl.when(member >= 0)
                    def _():
                        copy(tree, chunk, k, member).start()

        return carry

    lax.fori_loop(0, CHUNKS + 4 * LAG, step, 0)

    def drain(chunk, carry):
        for tree in range(3):
            for k in range(2):
                member = childs[tree][k]

                @pl.when(member >= 0)
                def _():
                    copy(tree, chunk, k, member).wait_send()

        return carry

    lax.fori_loop(0, CHUNKS, drain, 0)


def dress_kernel(table, slots, picks, cols, high, low, col_energy, row_energy, out, col_high, col_low, total):
    g = pl.program_id(0)
    vb, aux = lax.axis_index("vb"), lax.axis_index("aux")

    @pl.when(g == 0)
    def _():
        for q in range(4):
            block = (aux * 2 + q // 2) * NVB + vb * 2 + q % 2
            unpack(table, slots, lambda c: cols[q * BLK : (q + 1) * BLK, c], block, col_high, col_low, q * BLK)
        total[...] = jnp.zeros_like(total)

    ch, cl = col_high[...], col_low[...]
    parts_h, parts_l = [], []
    for i in range(2):
        rows = slice(i * TILE, (i + 1) * TILE)
        bh, bl = high[rows, :], low[rows, :]
        direct = dot_nt(ch, bh) + dot_nt(ch, bl) + dot_nt(cl, bh)
        energy = col_energy[...] + row_energy[0, i : i + 1, :]
        h, l = split(-direct / energy)
        parts_h.append(h)
        parts_l.append(l)
    th, tl = jnp.concatenate(parts_h, axis=1), jnp.concatenate(parts_l, axis=1)
    bh, bl = high[...], low[...]
    total[...] += dot_nn(th, bh) + dot_nn(th, bl) + dot_nn(tl, bh)

    @pl.when(g == 3)
    def _():
        for q in range(4):
            block = (aux * 2 + q // 2) * NVB + vb * 2 + q % 2
            rows = slice(q * BLK, (q + 1) * BLK)
            for k in range(PRESENT):
                pick = picks[block * NPB + k]
                out[rows, k * BLK : (k + 1) * BLK] = total[rows, pl.ds(pl.multiple_of(pick * BLK, BLK), BLK)]


def exchange_kernel(
    part, buf, relay, merged, recv,
    relay_s, relay_r, side_s, side_r, near_s, near_r, merge_s, merge_r,
    ag_s, ag_r, fwd_s, ex_s, ex_r, ring_s, ring_r, pair_s, pair_r,
):
    va, vb, aux = lax.axis_index("va"), lax.axis_index("vb"), lax.axis_index("aux")
    x, y = va // 2, va % 2
    core, hi = aux % 2, aux // 2
    right, left, across = (x + 1) % 4, (x + 3) % 4, (x + 2) % 4
    other = (aux + 2) % 4
    barrier = pltpu.get_barrier_semaphore()
    for k in range(1, 8):
        pl.semaphore_signal(barrier, 1, device_id={"va": (va + k) % 8}, device_id_type=MESH)
    pl.semaphore_signal(barrier, 1, device_id={"vb": (vb + 1) % 8}, device_id_type=MESH)
    pl.semaphore_signal(barrier, 1, device_id={"vb": (vb + 7) % 8}, device_id_type=MESH)
    partner = hi * 2 + (1 - core)
    pl.semaphore_signal(barrier, 1, device_id={"aux": partner}, device_id_type=MESH)

    @pl.when(va == vb)
    def _():
        for k in range(8):
            pl.semaphore_signal(barrier, 1, device_id={"va": (va + k) % 8, "aux": other}, device_id_type=MESH)

    pl.semaphore_wait(barrier, 11)

    def rows_of(owner, offset, size):
        return pl.ds(pl.multiple_of(owner * SLICE + offset, HALF), size)

    def put(src, dst, s, r, **device):
        return pltpu.make_async_remote_copy(src, dst, s, r, device_id=device, device_id_type=MESH)

    sends = []

    def go(copy):
        copy.start()
        sends.append(copy)

    for yy in range(2):
        far = across * 2 + yy
        go(put(part.at[rows_of(far, 0, HALF)], relay.at[0, yy], relay_s.at[0, yy], relay_r.at[0, yy], va=right * 2 + y))
        go(put(part.at[rows_of(far, HALF, HALF)], relay.at[1, yy], relay_s.at[1, yy], relay_r.at[1, yy], va=left * 2 + y))
    side = x * 2 + 1 - y
    go(put(part.at[rows_of(side, 0, SLICE)], recv.at[4], side_s, side_r, va=side))
    for yy in range(2):
        slot = (yy + y) % 2
        to_right, to_left = right * 2 + yy, left * 2 + yy
        go(put(part.at[rows_of(to_right, HALF, HALF)], recv.at[slot, pl.ds(HALF, HALF)], near_s.at[0, yy], near_r.at[slot], va=to_right))
        go(put(part.at[rows_of(to_left, 0, HALF)], recv.at[2 + slot, pl.ds(0, HALF)], near_s.at[1, yy], near_r.at[2 + slot], va=to_left))
    for yy in range(2):
        slot = (yy + y) % 2
        to_right, to_left = right * 2 + yy, left * 2 + yy
        put(relay.at[0, yy], relay.at[0, yy], relay_s.at[0, yy], relay_r.at[0, yy], va=va).wait_recv()
        merged[0, yy] = part[rows_of(to_right, 0, HALF)] + relay[0, yy]
        go(put(merged.at[0, yy], recv.at[slot, pl.ds(0, HALF)], merge_s.at[0, yy], merge_r.at[slot], va=to_right))
        put(relay.at[1, yy], relay.at[1, yy], relay_s.at[1, yy], relay_r.at[1, yy], va=va).wait_recv()
        merged[1, yy] = part[rows_of(to_left, HALF, HALF)] + relay[1, yy]
        go(put(merged.at[1, yy], recv.at[2 + slot, pl.ds(HALF, HALF)], merge_s.at[1, yy], merge_r.at[2 + slot], va=to_left))
    for slot in range(4):
        put(merged.at[0, 0], recv.at[slot, pl.ds(0, HALF)], near_s.at[0, 0], near_r.at[slot], va=va).wait_recv()
        put(merged.at[0, 0], recv.at[slot, pl.ds(0, HALF)], near_s.at[0, 0], merge_r.at[slot], va=va).wait_recv()
    put(recv.at[4], recv.at[4], side_s, side_r, va=va).wait_recv()

    mine = rows_of(va, 0, SLICE)

    def home(member):
        return jnp.where(member == vb, aux, 4)

    here = home(va)
    buf[here, mine] = part[mine] + ((recv[0] + recv[1]) + (recv[2] + recv[3])) + recv[4]

    own = buf.at[here, mine]
    targets = (right * 2 + y, left * 2 + y, x * 2 + 1 - y, right * 2 + 1 - y, left * 2 + 1 - y)
    for n, target in enumerate(targets):
        go(put(own, buf.at[home(target), mine], ag_s.at[n], ag_r.at[va, 0], va=target))
    go(put(own, buf.at[aux, mine], ex_s, ex_r.at[va], va=vb, aux=other))

    def arrived(owner, offset, size, part_index):
        ref = buf.at[here, rows_of(owner, offset, size)]
        put(ref, ref, ex_s, ag_r.at[owner, part_index], va=va).wait_recv()

    for n, yy in enumerate((y, 1 - y)):
        from_left, from_right = left * 2 + yy, right * 2 + yy
        arrived(from_left, 0, SLICE, 0)
        rows = rows_of(from_left, 0, HALF)
        go(put(buf.at[here, rows], buf.at[home(right * 2 + y), rows], fwd_s.at[0, n], ag_r.at[from_left, 0], va=right * 2 + y))
        arrived(from_right, 0, SLICE, 0)
        rows = rows_of(from_right, HALF, HALF)
        go(put(buf.at[here, rows], buf.at[home(left * 2 + y), rows], fwd_s.at[1, n], ag_r.at[from_right, 1], va=left * 2 + y))
    arrived(side, 0, SLICE, 0)
    for yy in range(2):
        arrived(across * 2 + yy, 0, HALF, 0)
        arrived(across * 2 + yy, HALF, HALF, 1)

    up, down = (vb + 1) % 8, (vb + 7) % 8
    distances = ((vb - va + 8) % 8, (va - vb + 8) % 8)
    owners = (va, side, *(m * 2 + yy for m in (right, left, across) for yy in (y, 1 - y)))

    def ring(step, way, what):
        h = step // 8
        owner = step % 8
        slice_owner = owners[7]
        for n in range(7):
            slice_owner = jnp.where(owner == n, owners[n], slice_owner)
        group = (hi + h) % 2
        ref = buf.at[group * 2 + core, rows_of(slice_owner, way * HALF, HALF)]
        if what == "ring":
            return put(ref, ref, ring_s.at[way, step], ring_r.at[way, step], vb=(up, down)[way])
        if what == "pair":
            return put(ref, ref, pair_s.at[way, step], pair_r.at[way, step], aux=partner)
        if what == "paired":
            other_ref = buf.at[group * 2 + 1 - core, rows_of(slice_owner, way * HALF, HALF)]
            return put(other_ref, other_ref, pair_s.at[way, step], pair_r.at[way, step], aux=partner)
        whole = buf.at[group * 2 + core, rows_of(slice_owner, 0, SLICE)]
        return put(whole, whole, ex_s, ex_r.at[slice_owner], vb=up)

    lags = [(RING_LAG * d) // 2 for d in distances]

    def ring_step(t, carry):
        for way in range(2):
            step = t - lags[way]

            @pl.when((step >= 0) & (step < 16))
            def _():
                @pl.when(va != vb)
                def _():
                    ring(step, way, "ring").wait_recv()

                if way == 0:

                    @pl.when((va == vb) & (step >= 8))
                    def _():
                        ring(step, way, "ex").wait_recv()

                @pl.when(distances[way] < 7)
                def _():
                    ring(step, way, "ring").start()

                ring(step, way, "pair").start()

        return carry

    lax.fori_loop(0, 16 + (RING_LAG * 7) // 2, ring_step, 0)

    def ring_drain(step, carry):
        for way in range(2):
            ring(step, way, "paired").wait_recv()
            ring(step, way, "pair").wait_send()

            @pl.when(distances[way] < 7)
            def _():
                ring(step, way, "ring").wait_send()

        return carry

    lax.fori_loop(0, 16, ring_drain, 0)

    for copy in sends:
        copy.wait_send()


def residual_kernel(where, table, slots, own, dressed, cols, col_dressed, row_energy, col_energy, out, row_high, row_low, col_high, col_low):
    g = pl.program_id(0)
    va, vb, aux = lax.axis_index("va"), lax.axis_index("vb"), lax.axis_index("aux")

    @pl.when(g == 0)
    def _():
        for q in range(4):
            block = (aux * 2 + q // 2) * NVB + vb * 2 + q % 2
            rows = slice(q * BLK, (q + 1) * BLK)
            unpack(table, slots, lambda c: cols[rows, c] + 2.0 * col_dressed[0, rows, c], block, col_high, col_low, q * BLK)

    for q in range(4):
        block = (g * 2 + q // 2) * NVB + va * 2 + q % 2
        rows = slice(q * BLK, (q + 1) * BLK)
        unpack(table, slots, lambda c: own[rows, c] + 2.0 * dressed[0, rows, c], block, row_high, row_low, q * BLK)
    ch, cl = col_high[...], col_low[...]
    for i in range(2):
        rows = slice(i * TILE, (i + 1) * TILE)
        rh, rl = row_high[rows, :], row_low[rows, :]
        total = dot_nt(rh, ch) + dot_nt(rh, cl) + dot_nt(rl, ch)
        result = -total / (row_energy[rows, :] + col_energy[...]) * SCALE
        out[i, :, 0, :] = result[:, :TILE]
        out[i, :, 1, :] = result[:, TILE:]


def body(factors, domains, occ_energy, vir_energy):
    va, vb, aux = lax.axis_index("va"), lax.axis_index("vb"), lax.axis_index("aux")
    blocks = jnp.arange(NPB, dtype=jnp.int32)
    slot_of = jnp.sum(jnp.where(blocks[:, None] > blocks[None, :], domains[:, :, None, :], 0), axis=-1)
    pick_of = jnp.sum(
        jnp.where((slot_of[:, :, None, :] == blocks[:, None]) & (domains[:, :, None, :] > 0), blocks, 0), axis=-1
    )
    table, slots, picks = domains.reshape(-1), slot_of.reshape(-1), pick_of.reshape(-1)
    vir_rows = lax.dynamic_slice_in_dim(vir_energy, va * TILE, TILE)
    vir_cols = lax.dynamic_slice_in_dim(vir_energy, vb * TILE, TILE)
    occ_cols = lax.dynamic_slice_in_dim(occ_energy, aux * 2, 2)
    row_energy = vir_rows[None, :] - occ_energy[:, None]
    col_energy = (vir_cols[None, :] - occ_cols[:, None]).reshape(PAIR)

    smem = pl.BlockSpec(memory_space=pltpu.SMEM)
    vmem = pl.BlockSpec(memory_space=pltpu.VMEM)
    whole = lambda shape: pl.BlockSpec(shape, lambda g: (0,) * len(shape))

    high, low, packed = pl.pallas_call(
        prep_kernel,
        grid=(NPB,),
        out_shape=(
            jax.ShapeDtypeStruct((ROWS, NAUX), BF16),
            jax.ShapeDtypeStruct((ROWS, NAUX), BF16),
            jax.ShapeDtypeStruct((ROWS, PACK), F32),
        ),
        in_specs=[smem, smem, pl.BlockSpec((BLK * O, BLK), lambda p: (p, 0)), pl.BlockSpec((BLK * O, BLK), lambda p: (p, 1))],
        out_specs=[
            pl.BlockSpec((ROWS, BLK), lambda p: (0, p)),
            pl.BlockSpec((ROWS, BLK), lambda p: (0, p)),
            whole((ROWS, PACK)),
        ],
        compiler_params=pltpu.CompilerParams(vmem_limit_bytes=VMEM_LIMIT),
        name="prep",
    )(table, slots, factors.reshape(NAUX * O, TILE), factors.reshape(NAUX * O, TILE))

    cols = pl.pallas_call(
        spread_kernel,
        out_shape=jax.ShapeDtypeStruct((PAIR, PACK), F32),
        in_specs=[pl.BlockSpec(memory_space=pl.ANY)],
        out_specs=vmem,
        scratch_shapes=[
            pltpu.SemaphoreType.DMA((3, CHUNKS, 2)),
            pltpu.SemaphoreType.DMA((3, CHUNKS)),
            pltpu.SemaphoreType.DMA,
        ],
        compiler_params=pltpu.CompilerParams(collective_id=0, has_side_effects=True, vmem_limit_bytes=VMEM_LIMIT),
        name="spread",
    )(packed)

    part = pl.pallas_call(
        dress_kernel,
        grid=(4,),
        out_shape=jax.ShapeDtypeStruct((PAIR, PACK), F32),
        in_specs=[
            smem, smem, smem,
            whole((PAIR, PACK)),
            pl.BlockSpec((PAIR, NAUX), lambda g: (g, 0)),
            pl.BlockSpec((PAIR, NAUX), lambda g: (g, 0)),
            whole((PAIR, 1)),
            pl.BlockSpec((1, 2, TILE), lambda g: (g, 0, 0)),
        ],
        out_specs=whole((PAIR, PACK)),
        scratch_shapes=[
            pltpu.VMEM((PAIR, NAUX), BF16),
            pltpu.VMEM((PAIR, NAUX), BF16),
            pltpu.VMEM((PAIR, NAUX), F32),
        ],
        compiler_params=pltpu.CompilerParams(vmem_limit_bytes=VMEM_LIMIT),
        name="dress",
    )(table, slots, picks, cols, high, low, col_energy.reshape(PAIR, 1), row_energy.reshape(4, 2, TILE))

    dma = pltpu.SemaphoreType.DMA
    buf = pl.pallas_call(
        exchange_kernel,
        out_shape=jax.ShapeDtypeStruct((5, PAIR, PACK), F32),
        in_specs=[vmem],
        out_specs=vmem,
        scratch_shapes=[
            pltpu.VMEM((2, 2, HALF, PACK), F32),
            pltpu.VMEM((2, 2, HALF, PACK), F32),
            pltpu.VMEM((5, SLICE, PACK), F32),
            dma((2, 2)), dma((2, 2)), dma, dma, dma((2, 2)), dma((4,)), dma((2, 2)), dma((4,)),
            dma((5,)), dma((8, 2)), dma((2, 2)), dma, dma((8,)), dma((2, 16)), dma((2, 16)), dma((2, 16)), dma((2, 16)),
        ],
        compiler_params=pltpu.CompilerParams(collective_id=1, has_side_effects=True, vmem_limit_bytes=VMEM_LIMIT),
        name="exchange",
    )(part)

    where = jnp.where(va == vb, aux, 4).astype(jnp.int32).reshape(1)
    return pl.pallas_call(
        residual_kernel,
        grid_spec=pltpu.PrefetchScalarGridSpec(
            num_scalar_prefetch=1,
            grid=(4,),
            in_specs=[
                smem, smem,
                pl.BlockSpec((PAIR, PACK), lambda g, w: (g, 0)),
                pl.BlockSpec((1, PAIR, PACK), lambda g, w: (g, 0, 0)),
                pl.BlockSpec((PAIR, PACK), lambda g, w: (0, 0)),
                pl.BlockSpec((1, PAIR, PACK), lambda g, w: (w[0], 0, 0)),
                pl.BlockSpec((PAIR, 1), lambda g, w: (g, 0)),
                pl.BlockSpec((1, PAIR), lambda g, w: (0, 0)),
            ],
            out_specs=pl.BlockSpec((2, TILE, 2, TILE), lambda g, w: (g, 0, 0, 0)),
            scratch_shapes=[pltpu.VMEM((PAIR, NAUX), BF16)] * 4,
        ),
        out_shape=jax.ShapeDtypeStruct((O, TILE, 2, TILE), F32),
        compiler_params=pltpu.CompilerParams(vmem_limit_bytes=VMEM_LIMIT),
        name="residual",
    )(where, table, slots, packed, buf, cols, buf, row_energy.reshape(ROWS, 1), col_energy.reshape(1, PAIR))


def solution(mesh):
    placed = (P(None, None, "va"), P(), P(), P())
    return jax.shard_map(
        body, mesh=mesh, in_specs=placed, out_specs=P(None, "va", "aux", "vb"), check_vma=False
    )
```

```python
import math

import jax
import jax.numpy as jnp
from jax import lax
from jax.experimental import pallas as pl
from jax.experimental.pallas import tpu as pltpu
from jax.sharding import PartitionSpec as P

O = 8
V = 2048
NAUX = 1024
BLK = 128
PRESENT = 6
NPB = 8
NVB = 16
TILE = 256
ROWS = O * TILE
PAIR = 2 * TILE
PACK = PRESENT * BLK
SLICE = PAIR // 8
HALF = SLICE // 2
CHUNKS = 8
STEPS = 16
LAG = 2
RING_LAG = 4
SCALE = 8.0 * O * V / math.sqrt(NAUX)
MESH = pl.DeviceIdType.MESH
F32 = jnp.float32
BF16 = jnp.bfloat16
VMEM_LIMIT = 60 * 1024 * 1024

TREES = (
    {0: (1,), 1: (2, 5), 2: (3, 6), 5: (4,), 6: (7,)},
    {0: (3,), 3: (2, 7), 2: (1,), 7: (4, 6), 6: (5,)},
    {0: (4,), 4: (5, 7), 5: (6, 1), 6: (2,), 7: (3,)},
)


def split(value):
    high = value.astype(BF16)
    return high, (value - high.astype(F32)).astype(BF16)


def dot_nt(left, right):
    return lax.dot_general(left, right, (((1,), (1,)), ((), ())), preferred_element_type=F32)


def dot_nn(left, right):
    return lax.dot_general(left, right, (((1,), (0,)), ((), ())), preferred_element_type=F32)


def kernel(
    domains, occ, vir, factors, out,
    raw, high, low, cols, col_high, col_low, total, part, buf, relay, merged, recv, row_high, row_low,
    row_weights, col_weights,
    load, spread_s, spread_r,
    relay_s, relay_r, side_s, side_r, near_s, near_r, merge_s, merge_r,
    ag_s, ag_r, fwd_s, ring_s, ring_r, pair_s, pair_r, far_s, far_r, last_s, last_r,
):
    va, vb, aux = lax.axis_index("va"), lax.axis_index("vb"), lax.axis_index("aux")
    x, y = va // 2, va % 2
    core, hi = aux % 2, aux // 2
    right, left, across = (x + 1) % 4, (x + 3) % 4, (x + 2) % 4
    partner, far, corner = hi * 2 + (1 - core), (aux + 2) % 4, ((1 - hi) * 2) + (1 - core)

    barrier = pltpu.get_barrier_semaphore()
    for k in range(1, 8):
        pl.semaphore_signal(barrier, 1, device_id={"va": (va + k) % 8}, device_id_type=MESH)
    pl.semaphore_signal(barrier, 1, device_id={"vb": (vb + 1) % 8}, device_id_type=MESH)
    pl.semaphore_signal(barrier, 1, device_id={"vb": (vb + 7) % 8}, device_id_type=MESH)
    pl.semaphore_signal(barrier, 1, device_id={"aux": partner}, device_id_type=MESH)
    pl.semaphore_signal(barrier, 1, device_id={"aux": far}, device_id_type=MESH)

    def fetch(p, half):
        rows = pl.ds(p * BLK * O, BLK * O)
        return pltpu.make_async_copy(factors.at[rows, pl.ds(half * BLK, BLK)], raw.at[half, rows], load.at[p, half])

    for p in range(NPB):
        for half in range(2):
            fetch(p, half).start()

    def weigh(table, n, i, block):
        absent = jnp.float32(0)
        for p in range(NPB):
            keep = domains[i, block, p].astype(F32)
            table[(n * NPB + p) * 3] = keep * (1.0 - absent) * (2.0 - absent) * 0.5
            table[(n * NPB + p) * 3 + 1] = keep * absent * (2.0 - absent)
            table[(n * NPB + p) * 3 + 2] = keep * absent * (absent - 1.0) * 0.5
            absent += 1.0 - keep

    def row_tables(n, carry):
        weigh(row_weights, n, n // 2, va * 2 + n % 2)
        return carry

    def col_tables(n, carry):
        weigh(col_weights, n, aux * 2 + n // 2, vb * 2 + n % 2)
        return carry

    lax.fori_loop(0, O * 2, row_tables, 0)
    lax.fori_loop(0, 4, col_tables, 0)

    def slot_of(n, k, full):
        values = [col_weights[(n * NPB + k + d) * 3 + d] * full(k + d) for d in range(3)]
        return values[0] + values[1] + values[2]

    def block_of(table, n, p, slots):
        values = [table[(n * NPB + p) * 3 + d] * slots(p - d) for d in range(3) if 0 <= p - d < PRESENT]
        return sum(values[1:], values[0])

    def lanes(slot):
        return pl.ds(pl.multiple_of(slot * BLK, BLK), BLK)

    def turned(i, half, p):
        keep = domains[i, va * 2 + half, p].astype(F32)
        return raw[half, pl.ds(p * (BLK * O) + i, BLK, stride=O), :].T * keep

    root_x, root_y = vb // 2, vb % 2
    node = (x - root_x + 4) % 4 + 4 * ((y + root_y) % 2)

    for p in range(NPB):
        for half in range(2):
            fetch(p, half).wait()

    @pl.when(node == 0)
    def _():
        def own(n, carry):
            i, half = aux * 2 + n // 2, n % 2
            rows = pl.ds(pl.multiple_of(n * BLK, BLK), BLK)
            for p in range(NPB):
                total[rows, p * BLK : (p + 1) * BLK] = turned(i, half, p)
            for k in range(PRESENT):
                cols[rows, k * BLK : (k + 1) * BLK] = slot_of(n, k, lambda p: total[rows, p * BLK : (p + 1) * BLK])
            return carry

        lax.fori_loop(0, 4, own, 0)

    def lookup(values):
        found = jnp.int32(values[0])
        for n in range(1, 8):
            found = jnp.where(node == n, jnp.int32(values[n]), found)
        return found

    skews, childs = [], []
    for tree in TREES:
        depth = {0: 0}
        todo = [0]
        for n in todo:
            for member in tree.get(n, ()):
                depth[member] = depth[n] + 1
                todo.append(member)
        skews.append(lookup([LAG * depth[n] for n in range(8)]))
        childs.append([lookup([(*tree.get(n, ()), -1, -1)[k] for n in range(8)]) for k in range(2)])

    def spread(tree, chunk, child, member):
        ref = cols.at[pl.ds(pl.multiple_of(chunk * SLICE, SLICE), SLICE), pl.ds(tree * 256, 256)]
        place = ((root_x + member % 4) % 4) * 2 + (root_y + member // 4) % 2
        return pltpu.make_async_remote_copy(
            ref, ref, spread_s.at[tree, chunk, child], spread_r.at[tree, chunk], device_id={"va": place}, device_id_type=MESH
        )

    pl.semaphore_wait(barrier, 11)

    def step(t, carry):
        for tree in range(3):
            chunk = t - skews[tree]

            @pl.when((chunk >= 0) & (chunk < CHUNKS))
            def _():
                @pl.when(node != 0)
                def _():
                    spread(tree, chunk, 0, 0).wait_recv()

                for k in range(2):
                    member = childs[tree][k]

                    @pl.when(member >= 0)
                    def _():
                        spread(tree, chunk, k, member).start()

        p = t // 2
        for n in range(4):
            i = (t % 2) * 4 + n
            for half in range(2):
                h, l = split(turned(i, half, p))
                rows = pl.ds(pl.multiple_of(i * TILE + half * BLK, BLK), BLK)
                high[rows, lanes(p)] = h
                low[rows, lanes(p)] = l
        return carry

    lax.fori_loop(0, STEPS, step, 0)

    def spread_drain(chunk, carry):
        for tree in range(3):
            for k in range(2):
                member = childs[tree][k]

                @pl.when(member >= 0)
                def _():
                    spread(tree, chunk, k, member).wait_send()

        return carry

    def energy_row(tile):
        return [vir[pl.ds(tile * 2 + half, 1), :] for half in range(2)]

    def energy_column(rows):
        return jnp.concatenate([jnp.broadcast_to(row, (8, BLK)).T[:, :1] for row in rows], axis=0)

    rows_a, rows_b = energy_row(va), energy_row(vb)
    row_a = jnp.concatenate(rows_a, axis=1)
    occ_j = [occ[aux * 2 + j] for j in range(2)]
    row_b = jnp.concatenate([row - occ_j[j] for j in range(2) for row in rows_b], axis=1)
    column_a = energy_column(rows_a)
    column_b = energy_column([row - occ_j[j] for j in range(2) for row in rows_b])

    def col_unpack(n, extra):
        rows = pl.ds(pl.multiple_of(n * BLK, BLK), BLK)
        for p in range(NPB):
            h, l = split(block_of(col_weights, n, p, lambda s: extra(rows, slice(s * BLK, (s + 1) * BLK))))
            col_high[rows, p * BLK : (p + 1) * BLK] = h
            col_low[rows, p * BLK : (p + 1) * BLK] = l

    def first_cols(n, carry):
        col_unpack(n, lambda rows, there: cols[rows, there])
        return carry

    lax.fori_loop(0, 4, first_cols, 0)
    total[...] = jnp.zeros_like(total)

    def dress(g, carry):
        ch, cl = col_high[...], col_low[...]
        parts_h, parts_l = [], []
        for i in range(2):
            rows = pl.ds(pl.multiple_of(g * PAIR + i * TILE, TILE), TILE)
            bh, bl = high[rows, :], low[rows, :]
            direct = dot_nt(ch, bh) + dot_nt(ch, bl) + dot_nt(cl, bh)
            energy = column_b + (row_a - occ[g * 2 + i])
            h, l = split(-direct / energy)
            parts_h.append(h)
            parts_l.append(l)
        th, tl = jnp.concatenate(parts_h, axis=1), jnp.concatenate(parts_l, axis=1)
        rows = pl.ds(pl.multiple_of(g * PAIR, PAIR), PAIR)
        bh, bl = high[rows, :], low[rows, :]
        total[...] += dot_nn(th, bh) + dot_nn(th, bl) + dot_nn(tl, bh)
        return carry

    lax.fori_loop(0, 4, dress, 0)

    def pack(n, carry):
        rows = pl.ds(pl.multiple_of(n * BLK, BLK), BLK)
        for k in range(PRESENT):
            part[rows, k * BLK : (k + 1) * BLK] = slot_of(n, k, lambda p: total[rows, p * BLK : (p + 1) * BLK])
        return carry

    lax.fori_loop(0, 4, pack, 0)

    def rows_of(owner, offset, size):
        return pl.ds(pl.multiple_of(owner * SLICE + offset, HALF), size)

    def put(src, dst, s, r, **device):
        return pltpu.make_async_remote_copy(src, dst, s, r, device_id=device, device_id_type=MESH)

    sends = []

    def go(copy):
        copy.start()
        sends.append(copy)

    for yy in range(2):
        opposite = across * 2 + yy
        go(put(part.at[rows_of(opposite, 0, HALF)], relay.at[0, yy], relay_s.at[0, yy], relay_r.at[0, yy], va=right * 2 + y))
        go(put(part.at[rows_of(opposite, HALF, HALF)], relay.at[1, yy], relay_s.at[1, yy], relay_r.at[1, yy], va=left * 2 + y))
    side = x * 2 + 1 - y
    go(put(part.at[rows_of(side, 0, SLICE)], recv.at[4], side_s, side_r, va=side))
    for yy in range(2):
        slot = (yy + y) % 2
        to_right, to_left = right * 2 + yy, left * 2 + yy
        go(put(part.at[rows_of(to_right, HALF, HALF)], recv.at[slot, pl.ds(HALF, HALF)], near_s.at[0, yy], near_r.at[slot], va=to_right))
        go(put(part.at[rows_of(to_left, 0, HALF)], recv.at[2 + slot, pl.ds(0, HALF)], near_s.at[1, yy], near_r.at[2 + slot], va=to_left))
    for yy in range(2):
        slot = (yy + y) % 2
        to_right, to_left = right * 2 + yy, left * 2 + yy
        put(relay.at[0, yy], relay.at[0, yy], relay_s.at[0, yy], relay_r.at[0, yy], va=va).wait_recv()
        merged[0, yy] = part[rows_of(to_right, 0, HALF)] + relay[0, yy]
        go(put(merged.at[0, yy], recv.at[slot, pl.ds(0, HALF)], merge_s.at[0, yy], merge_r.at[slot], va=to_right))
        put(relay.at[1, yy], relay.at[1, yy], relay_s.at[1, yy], relay_r.at[1, yy], va=va).wait_recv()
        merged[1, yy] = part[rows_of(to_left, HALF, HALF)] + relay[1, yy]
        go(put(merged.at[1, yy], recv.at[2 + slot, pl.ds(HALF, HALF)], merge_s.at[1, yy], merge_r.at[2 + slot], va=to_left))
    for slot in range(4):
        put(merged.at[0, 0], recv.at[slot, pl.ds(0, HALF)], near_s.at[0, 0], near_r.at[slot], va=va).wait_recv()
        put(merged.at[0, 0], recv.at[slot, pl.ds(0, HALF)], near_s.at[0, 0], merge_r.at[slot], va=va).wait_recv()
    put(recv.at[4], recv.at[4], side_s, side_r, va=va).wait_recv()

    mine = rows_of(va, 0, SLICE)

    def home(member):
        return jnp.where(member == vb, aux, 4)

    here = home(va)
    buf[here, mine] = part[mine] + ((recv[0] + recv[1]) + (recv[2] + recv[3])) + recv[4]

    own = buf.at[here, mine]
    targets = (right * 2 + y, left * 2 + y, x * 2 + 1 - y, right * 2 + 1 - y, left * 2 + 1 - y)
    for n, target in enumerate(targets):
        go(put(own, buf.at[home(target), mine], ag_s.at[n], ag_r.at[va, 0], va=target))

    def arrived(owner, offset, size, part_index):
        ref = buf.at[here, rows_of(owner, offset, size)]
        put(ref, ref, side_s, ag_r.at[owner, part_index], va=va).wait_recv()

    for n, yy in enumerate((y, 1 - y)):
        from_left, from_right = left * 2 + yy, right * 2 + yy
        arrived(from_left, 0, SLICE, 0)
        rows = rows_of(from_left, 0, HALF)
        go(put(buf.at[here, rows], buf.at[home(right * 2 + y), rows], fwd_s.at[0, n], ag_r.at[from_left, 0], va=right * 2 + y))
        arrived(from_right, 0, SLICE, 0)
        rows = rows_of(from_right, HALF, HALF)
        go(put(buf.at[here, rows], buf.at[home(left * 2 + y), rows], fwd_s.at[1, n], ag_r.at[from_right, 1], va=left * 2 + y))
    arrived(side, 0, SLICE, 0)
    for yy in range(2):
        arrived(across * 2 + yy, 0, HALF, 0)
        arrived(across * 2 + yy, HALF, HALF, 1)

    up, down = (vb + 1) % 8, (vb + 7) % 8
    distances = ((vb - va + 8) % 8, (va - vb + 8) % 8)
    owners = (va, side, *(m * 2 + yy for m in (right, left, across) for yy in (y, 1 - y)))

    def chunk_rows(step, way):
        owner = owners[7]
        for n in range(7):
            owner = jnp.where(step == n, owners[n], owner)
        return rows_of(owner, way * HALF, HALF)

    def ring(group, step, way, sems, **device):
        ref = buf.at[group, chunk_rows(step, way)]
        return put(ref, ref, sems[0].at[way, step], sems[1].at[way, step], **device)

    ring_sems, pair_sems, far_sems, last_sems = (ring_s, ring_r), (pair_s, pair_r), (far_s, far_r), (last_s, last_r)
    lags = [(RING_LAG * d) // 2 for d in distances]

    def ring_step(t, carry):
        for way in range(2):
            step = t - lags[way]
            toward = (up, down)[way]

            @pl.when((step >= 0) & (step < 8))
            def _():
                @pl.when(va != vb)
                def _():
                    ring(aux, step, way, ring_sems, va=va).wait_recv()

                @pl.when(distances[way] < 7)
                def _():
                    ring(aux, step, way, ring_sems, vb=toward).start()

                ring(aux, step, way, far_sems, aux=far).start()
                ring(aux, step, way, pair_sems, aux=partner).start()

        return carry

    lax.fori_loop(0, 8 + (RING_LAG * 7) // 2, ring_step, 0)

    def second_cols(n, carry):
        col_unpack(n, lambda rows, there: cols[rows, there] + 2.0 * buf[here, rows, there])
        return carry

    lax.fori_loop(0, 4, second_cols, 0)

    def residual(group):
        for i in range(2):
            orbital = group * 2 + i
            for half in range(2):
                rows = pl.ds(pl.multiple_of(orbital * TILE + half * BLK, BLK), BLK)
                here_rows = pl.ds(i * TILE + half * BLK, BLK)
                for p in range(NPB):
                    block = slice(p * BLK, (p + 1) * BLK)
                    value = high[rows, block].astype(F32) + low[rows, block].astype(F32)
                    change = block_of(
                        row_weights, orbital * 2 + half, p, lambda s: buf[group, here_rows, s * BLK : (s + 1) * BLK]
                    )
                    h, l = split(value + 2.0 * change)
                    row_high[half * BLK : (half + 1) * BLK, block] = h
                    row_low[half * BLK : (half + 1) * BLK, block] = l
            rh, rl = row_high[...], row_low[...]
            ch, cl = col_high[...], col_low[...]
            result = dot_nt(rh, ch) + dot_nt(rh, cl) + dot_nt(rl, ch)
            result = -result / ((column_a - occ[orbital]) + row_b) * SCALE
            out[orbital, :, 0, :] = result[:, :TILE]
            out[orbital, :, 1, :] = result[:, TILE:]

    def wait_chunks(group, sems):
        def one(step, carry):
            for way in range(2):
                ring(group, step, way, sems, va=va).wait_recv()
            return carry

        lax.fori_loop(0, 8, one, 0)

    def phase(n, carry):
        group = jnp.where(n == 0, aux, jnp.where(n == 1, partner, jnp.where(n == 2, far, corner)))

        @pl.when(n == 1)
        def _():
            wait_chunks(partner, pair_sems)

        @pl.when(n == 2)
        def _():
            def onward(step, carry):
                for way in range(2):
                    ring(far, step, way, far_sems, va=va).wait_recv()
                    ring(far, step, way, last_sems, aux=partner).start()
                return carry

            lax.fori_loop(0, 8, onward, 0)

        @pl.when(n == 3)
        def _():
            wait_chunks(corner, last_sems)

        residual(group)
        return carry

    lax.fori_loop(0, 4, phase, 0)

    def ring_drain(step, carry):
        for way in range(2):
            ring(aux, step, way, pair_sems, aux=partner).wait_send()
            ring(aux, step, way, far_sems, aux=far).wait_send()
            ring(far, step, way, last_sems, aux=partner).wait_send()

            @pl.when(distances[way] < 7)
            def _():
                ring(aux, step, way, ring_sems, vb=up).wait_send()

        return carry

    lax.fori_loop(0, 8, ring_drain, 0)
    lax.fori_loop(0, CHUNKS, spread_drain, 0)
    for copy in sends:
        copy.wait_send()


def body(factors, domains, occ_energy, vir_energy):
    smem = pl.BlockSpec(memory_space=pltpu.SMEM)
    vmem = pl.BlockSpec(memory_space=pltpu.VMEM)
    dma = pltpu.SemaphoreType.DMA
    return pl.pallas_call(
        kernel,
        out_shape=jax.ShapeDtypeStruct((O, TILE, 2, TILE), F32),
        in_specs=[smem, smem, vmem, pl.BlockSpec(memory_space=pl.ANY)],
        out_specs=vmem,
        scratch_shapes=[
            pltpu.VMEM((2, NAUX * O, BLK), F32),
            pltpu.VMEM((ROWS, NAUX), BF16),
            pltpu.VMEM((ROWS, NAUX), BF16),
            pltpu.VMEM((PAIR, PACK), F32),
            pltpu.VMEM((PAIR, NAUX), BF16),
            pltpu.VMEM((PAIR, NAUX), BF16),
            pltpu.VMEM((PAIR, NAUX), F32),
            pltpu.VMEM((PAIR, PACK), F32),
            pltpu.VMEM((5, PAIR, PACK), F32),
            pltpu.VMEM((2, 2, HALF, PACK), F32),
            pltpu.VMEM((2, 2, HALF, PACK), F32),
            pltpu.VMEM((5, SLICE, PACK), F32),
            pltpu.VMEM((TILE, NAUX), BF16),
            pltpu.VMEM((TILE, NAUX), BF16),
            pltpu.SMEM((O * 2 * NPB * 3,), F32),
            pltpu.SMEM((4 * NPB * 3,), F32),
            dma((NPB, 2)), dma((3, CHUNKS, 2)), dma((3, CHUNKS)),
            dma((2, 2)), dma((2, 2)), dma, dma, dma((2, 2)), dma((4,)), dma((2, 2)), dma((4,)),
            dma((5,)), dma((8, 2)), dma((2, 2)),
            dma((2, 8)), dma((2, 8)), dma((2, 8)), dma((2, 8)), dma((2, 8)), dma((2, 8)), dma((2, 8)), dma((2, 8)),
        ],
        compiler_params=pltpu.CompilerParams(collective_id=0, has_side_effects=True, vmem_limit_bytes=VMEM_LIMIT),
        name="amplitudes",
    )(domains, occ_energy, vir_energy.reshape(NVB, BLK), factors.reshape(NAUX * O, TILE))


def solution(mesh):
    placed = (P(None, None, "va"), P(), P(), P())
    return jax.shard_map(
        body, mesh=mesh, in_specs=placed, out_specs=P(None, "va", "aux", "vb"), check_vma=False
    )
```

```python
import math

import jax
import jax.numpy as jnp
from jax import lax
from jax.experimental import pallas as pl
from jax.experimental.pallas import tpu as pltpu
from jax.sharding import PartitionSpec as P

O = 8
V = 2048
NAUX = 1024
BLK = 128
PRESENT = 6
NPB = 8
NVB = 16
TILE = 256
ROWS = O * TILE
PAIR = 2 * TILE
PACK = PRESENT * BLK
SLICE = PAIR // 8
HALF = SLICE // 2
CHUNKS = 8
STEPS = 16
LEAD = 5
EARLY = 3
LAG = 2
RING_LAG = 4
SCALE = 8.0 * O * V / math.sqrt(NAUX)
MESH = pl.DeviceIdType.MESH
F32 = jnp.float32
BF16 = jnp.bfloat16
VMEM_LIMIT = 60 * 1024 * 1024

TREES = (
    {0: (1,), 1: (2, 5), 2: (3, 6), 5: (4,), 6: (7,)},
    {0: (3,), 3: (2, 7), 2: (1,), 7: (4, 6), 6: (5,)},
    {0: (4,), 4: (5, 7), 5: (6, 1), 6: (2,), 7: (3,)},
)


def split(value):
    high = value.astype(BF16)
    return high, (value - high.astype(F32)).astype(BF16)


def dot_nt(left, right):
    return lax.dot_general(left, right, (((1,), (1,)), ((), ())), preferred_element_type=F32)


def dot_nn(left, right):
    return lax.dot_general(left, right, (((1,), (0,)), ((), ())), preferred_element_type=F32)


def kernel(
    domains, occ, vir, factors, out,
    raw, high, low, cols, col_high, col_low, total, part, buf, relay, merged, recv, row_high, row_low,
    row_weights, col_weights,
    load, spread_s, spread_r,
    relay_s, relay_r, side_s, side_r, near_s, near_r, merge_s, merge_r,
    ag_s, ag_r, fwd_s, ring_s, ring_r, pair_s, pair_r, far_s, far_r, last_s, last_r,
):
    va, vb, aux = lax.axis_index("va"), lax.axis_index("vb"), lax.axis_index("aux")
    x, y = va // 2, va % 2
    core, hi = aux % 2, aux // 2
    right, left, across = (x + 1) % 4, (x + 3) % 4, (x + 2) % 4
    partner, far, corner = hi * 2 + (1 - core), (aux + 2) % 4, ((1 - hi) * 2) + (1 - core)

    barrier = pltpu.get_barrier_semaphore()
    for k in range(1, 8):
        pl.semaphore_signal(barrier, 1, device_id={"va": (va + k) % 8}, device_id_type=MESH)
    pl.semaphore_signal(barrier, 1, device_id={"vb": (vb + 1) % 8}, device_id_type=MESH)
    pl.semaphore_signal(barrier, 1, device_id={"vb": (vb + 7) % 8}, device_id_type=MESH)
    pl.semaphore_signal(barrier, 1, device_id={"aux": partner}, device_id_type=MESH)
    pl.semaphore_signal(barrier, 1, device_id={"aux": far}, device_id_type=MESH)

    def fetch(p, half):
        rows = pl.ds(p * BLK * O, BLK * O)
        return pltpu.make_async_copy(factors.at[rows, pl.ds(half * BLK, BLK)], raw.at[half, rows], load.at[p, half])

    for p in range(NPB):
        for half in range(2):
            fetch(p, half).start()

    def weigh(table, n, i, block):
        absent = jnp.float32(0)
        for p in range(NPB):
            keep = domains[i, p, block].astype(F32)
            table[(n * NPB + p) * 3] = keep * (1.0 - absent) * (2.0 - absent) * 0.5
            table[(n * NPB + p) * 3 + 1] = keep * absent * (2.0 - absent)
            table[(n * NPB + p) * 3 + 2] = keep * absent * (absent - 1.0) * 0.5
            absent += 1.0 - keep

    def row_tables(n, carry):
        weigh(row_weights, n, n // 2, va * 2 + n % 2)
        return carry

    def col_tables(n, carry):
        weigh(col_weights, n, aux * 2 + n // 2, vb * 2 + n % 2)
        return carry

    lax.fori_loop(0, O * 2, row_tables, 0)
    lax.fori_loop(0, 4, col_tables, 0)

    def slot_of(n, k, full):
        values = [col_weights[(n * NPB + k + d) * 3 + d] * full(k + d) for d in range(3)]
        return values[0] + values[1] + values[2]

    def block_of(table, n, p, slots):
        values = [table[(n * NPB + p) * 3 + d] * slots(p - d) for d in range(3) if 0 <= p - d < PRESENT]
        return sum(values[1:], values[0])

    def lanes(slot):
        return pl.ds(pl.multiple_of(slot * BLK, BLK), BLK)

    def turned(i, half, p):
        keep = domains[i, p, va * 2 + half].astype(F32)
        return raw[half, pl.ds(p * (BLK * O) + i, BLK, stride=O), :].T * keep

    root_x, root_y = vb // 2, vb % 2
    node = (x - root_x + 4) % 4 + 4 * ((y + root_y) % 2)

    for p in range(NPB):
        for half in range(2):
            fetch(p, half).wait()

    @pl.when(node == 0)
    def _():
        def own(n, carry):
            i, half = aux * 2 + n // 2, n % 2
            rows = pl.ds(pl.multiple_of(n * BLK, BLK), BLK)
            for p in range(NPB):
                total[rows, p * BLK : (p + 1) * BLK] = turned(i, half, p)
            for k in range(PRESENT):
                cols[rows, k * BLK : (k + 1) * BLK] = slot_of(n, k, lambda p: total[rows, p * BLK : (p + 1) * BLK])
            return carry

        lax.fori_loop(0, 4, own, 0)

    def lookup(values):
        found = jnp.int32(values[0])
        for n in range(1, 8):
            found = jnp.where(node == n, jnp.int32(values[n]), found)
        return found

    skews, childs = [], []
    for tree in TREES:
        depth = {0: 0}
        todo = [0]
        for n in todo:
            for member in tree.get(n, ()):
                depth[member] = depth[n] + 1
                todo.append(member)
        skews.append(lookup([LEAD + LAG * (depth[n] - 1) for n in range(8)]))
        childs.append([lookup([(*tree.get(n, ()), -1, -1)[k] for n in range(8)]) for k in range(2)])

    def spread(tree, chunk, child, member):
        ref = cols.at[pl.ds(pl.multiple_of(chunk * SLICE, SLICE), SLICE), pl.ds(tree * 256, 256)]
        place = ((root_x + member % 4) % 4) * 2 + (root_y + member // 4) % 2
        return pltpu.make_async_remote_copy(
            ref, ref, spread_s.at[tree, chunk, child], spread_r.at[tree, chunk], device_id={"va": place}, device_id_type=MESH
        )

    pl.semaphore_wait(barrier, 11)

    @pl.when(node == 0)
    def _():
        def launch(chunk, carry):
            for tree in range(3):
                spread(tree, chunk, 0, childs[tree][0]).start()
            return carry

        lax.fori_loop(0, CHUNKS, launch, 0)

    def step(t, carry):
        for tree in range(3):
            chunk = t - skews[tree]

            @pl.when((node != 0) & (chunk >= 0) & (chunk < CHUNKS))
            def _():
                spread(tree, chunk, 0, 0).wait_recv()
                for k in range(2):
                    member = childs[tree][k]

                    @pl.when(member >= 0)
                    def _():
                        spread(tree, chunk, k, member).start()

        @pl.when(t < STEPS)
        def _():
            p = t // 2
            for n in range(4):
                i = (t % 2) * 4 + n
                for half in range(2):
                    h, l = split(turned(i, half, p))
                    rows = pl.ds(pl.multiple_of(i * TILE + half * BLK, BLK), BLK)
                    high[rows, lanes(p)] = h
                    low[rows, lanes(p)] = l

        return carry

    lax.fori_loop(0, LEAD + CHUNKS + 3 * LAG, step, 0)

    def spread_drain(chunk, carry):
        for tree in range(3):
            for k in range(2):
                member = childs[tree][k]

                @pl.when(member >= 0)
                def _():
                    spread(tree, chunk, k, member).wait_send()

        return carry

    def energy_row(tile):
        return [vir[pl.ds(tile * 2 + half, 1), :] for half in range(2)]

    def energy_column(rows):
        return jnp.concatenate([jnp.broadcast_to(row, (8, BLK)).T[:, :1] for row in rows], axis=0)

    rows_a, rows_b = energy_row(va), energy_row(vb)
    row_a = jnp.concatenate(rows_a, axis=1)
    occ_j = [occ[aux * 2 + j] for j in range(2)]
    row_b = jnp.concatenate([row - occ_j[j] for j in range(2) for row in rows_b], axis=1)
    column_a = energy_column(rows_a)
    column_b = energy_column([row - occ_j[j] for j in range(2) for row in rows_b])

    def col_unpack(n, extra):
        rows = pl.ds(pl.multiple_of(n * BLK, BLK), BLK)
        for p in range(NPB):
            h, l = split(block_of(col_weights, n, p, lambda s: extra(rows, slice(s * BLK, (s + 1) * BLK))))
            col_high[rows, p * BLK : (p + 1) * BLK] = h
            col_low[rows, p * BLK : (p + 1) * BLK] = l

    def first_cols(n, carry):
        col_unpack(n, lambda rows, there: cols[rows, there])
        return carry

    lax.fori_loop(0, 4, first_cols, 0)
    total[...] = jnp.zeros_like(total)

    def dress(g, carry):
        ch, cl = col_high[...], col_low[...]
        parts_h, parts_l = [], []
        for i in range(2):
            rows = pl.ds(pl.multiple_of(g * PAIR + i * TILE, TILE), TILE)
            bh, bl = high[rows, :], low[rows, :]
            direct = dot_nt(ch, bh) + dot_nt(ch, bl) + dot_nt(cl, bh)
            energy = column_b + (row_a - occ[g * 2 + i])
            h, l = split(-direct / energy)
            parts_h.append(h)
            parts_l.append(l)
        th, tl = jnp.concatenate(parts_h, axis=1), jnp.concatenate(parts_l, axis=1)
        rows = pl.ds(pl.multiple_of(g * PAIR, PAIR), PAIR)
        bh, bl = high[rows, :], low[rows, :]
        total[...] += dot_nn(th, bh) + dot_nn(th, bl) + dot_nn(tl, bh)
        return carry

    lax.fori_loop(0, 4, dress, 0)

    def pack(n, carry):
        rows = pl.ds(pl.multiple_of(n * BLK, BLK), BLK)
        for k in range(PRESENT):
            part[rows, k * BLK : (k + 1) * BLK] = slot_of(n, k, lambda p: total[rows, p * BLK : (p + 1) * BLK])
        return carry

    lax.fori_loop(0, 4, pack, 0)

    def rows_of(owner, offset, size):
        return pl.ds(pl.multiple_of(owner * SLICE + offset, HALF), size)

    def put(src, dst, s, r, **device):
        return pltpu.make_async_remote_copy(src, dst, s, r, device_id=device, device_id_type=MESH)

    sends = []

    def go(copy):
        copy.start()
        sends.append(copy)

    for yy in range(2):
        opposite = across * 2 + yy
        go(put(part.at[rows_of(opposite, 0, HALF)], relay.at[0, yy], relay_s.at[0, yy], relay_r.at[0, yy], va=right * 2 + y))
        go(put(part.at[rows_of(opposite, HALF, HALF)], relay.at[1, yy], relay_s.at[1, yy], relay_r.at[1, yy], va=left * 2 + y))
    side = x * 2 + 1 - y
    go(put(part.at[rows_of(side, 0, SLICE)], recv.at[4], side_s, side_r, va=side))
    for yy in range(2):
        slot = (yy + y) % 2
        to_right, to_left = right * 2 + yy, left * 2 + yy
        go(put(part.at[rows_of(to_right, HALF, HALF)], recv.at[slot, pl.ds(HALF, HALF)], near_s.at[0, yy], near_r.at[slot], va=to_right))
        go(put(part.at[rows_of(to_left, 0, HALF)], recv.at[2 + slot, pl.ds(0, HALF)], near_s.at[1, yy], near_r.at[2 + slot], va=to_left))
    for yy in range(2):
        slot = (yy + y) % 2
        to_right, to_left = right * 2 + yy, left * 2 + yy
        put(relay.at[0, yy], relay.at[0, yy], relay_s.at[0, yy], relay_r.at[0, yy], va=va).wait_recv()
        merged[0, yy] = part[rows_of(to_right, 0, HALF)] + relay[0, yy]
        go(put(merged.at[0, yy], recv.at[slot, pl.ds(0, HALF)], merge_s.at[0, yy], merge_r.at[slot], va=to_right))
        put(relay.at[1, yy], relay.at[1, yy], relay_s.at[1, yy], relay_r.at[1, yy], va=va).wait_recv()
        merged[1, yy] = part[rows_of(to_left, HALF, HALF)] + relay[1, yy]
        go(put(merged.at[1, yy], recv.at[2 + slot, pl.ds(HALF, HALF)], merge_s.at[1, yy], merge_r.at[2 + slot], va=to_left))
    for slot in range(4):
        put(merged.at[0, 0], recv.at[slot, pl.ds(0, HALF)], near_s.at[0, 0], near_r.at[slot], va=va).wait_recv()
        put(merged.at[0, 0], recv.at[slot, pl.ds(0, HALF)], near_s.at[0, 0], merge_r.at[slot], va=va).wait_recv()
    put(recv.at[4], recv.at[4], side_s, side_r, va=va).wait_recv()

    mine = rows_of(va, 0, SLICE)

    def home(member):
        return jnp.where(member == vb, aux, 4)

    here = home(va)
    buf[here, mine] = part[mine] + ((recv[0] + recv[1]) + (recv[2] + recv[3])) + recv[4]

    own = buf.at[here, mine]
    targets = (right * 2 + y, left * 2 + y, x * 2 + 1 - y, right * 2 + 1 - y, left * 2 + 1 - y)
    for n, target in enumerate(targets):
        go(put(own, buf.at[home(target), mine], ag_s.at[n], ag_r.at[va, 0], va=target))

    def arrived(owner, offset, size, part_index):
        ref = buf.at[here, rows_of(owner, offset, size)]
        put(ref, ref, side_s, ag_r.at[owner, part_index], va=va).wait_recv()

    up, down = (vb + 1) % 8, (vb + 7) % 8
    distances = ((vb - va + 8) % 8, (va - vb + 8) % 8)
    owners = (va, side, *(m * 2 + yy for m in (right, left, across) for yy in (y, 1 - y)))

    def chunk_rows(step, way):
        owner = owners[7]
        for n in range(7):
            owner = jnp.where(step == n, owners[n], owner)
        return rows_of(owner, way * HALF, HALF)

    def ring(group, step, way, sems, **device):
        ref = buf.at[group, chunk_rows(step, way)]
        return put(ref, ref, sems[0].at[way, step], sems[1].at[way, step], **device)

    pair_sems, far_sems, last_sems = (pair_s, pair_r), (far_s, far_r), (last_s, last_r)
    lags = [(RING_LAG * d) // 2 for d in distances]
    source = va == vb

    def ring_step(t, carry):
        for way in range(2):
            step = t - lags[way]
            toward = (up, down)[way]

            @pl.when((step >= 0) & (step < 8 + EARLY))
            def _():
                late = step >= 8
                local = jnp.where(late, step - 8, step)
                ref = buf.at[jnp.where(late, far, aux), chunk_rows(local, way)]
                along = put(ref, ref, ring_s.at[way, step], ring_r.at[way, step], vb=toward)

                @pl.when(jnp.logical_not(source))
                def _():
                    along.wait_recv()

                @pl.when(source & late)
                def _():
                    ring(far, local, way, far_sems, va=va).wait_recv()

                if way == 0:

                    @pl.when(source & (step == 1))
                    def _():
                        arrived(side, 0, SLICE, 0)

                    for n, yy in enumerate((y, 1 - y)):

                        @pl.when(source & (step == 6 + n))
                        def _():
                            arrived(across * 2 + yy, 0, HALF, 0)
                            arrived(across * 2 + yy, HALF, HALF, 1)

                @pl.when(distances[way] < 7)
                def _():
                    along.start()

                @pl.when(jnp.logical_not(late))
                def _():
                    @pl.when(source | (step >= EARLY))
                    def _():
                        ring(aux, local, way, far_sems, aux=far).start()

                    ring(aux, local, way, pair_sems, aux=partner).start()

                @pl.when(late)
                def _():
                    ring(far, local, way, last_sems, aux=partner).start()

        return carry

    @pl.when(source)
    def _():
        ring_step(0, 0)

    for n, yy in enumerate((y, 1 - y)):
        from_left, from_right = left * 2 + yy, right * 2 + yy
        arrived(from_left, 0, SLICE, 0)
        rows = rows_of(from_left, 0, HALF)
        go(put(buf.at[here, rows], buf.at[home(right * 2 + y), rows], fwd_s.at[0, n], ag_r.at[from_left, 0], va=right * 2 + y))
        arrived(from_right, 0, SLICE, 0)
        rows = rows_of(from_right, HALF, HALF)
        go(put(buf.at[here, rows], buf.at[home(left * 2 + y), rows], fwd_s.at[1, n], ag_r.at[from_right, 1], va=left * 2 + y))
    lax.fori_loop(1, 8 + EARLY + (RING_LAG * 7) // 2, ring_step, 0)

    @pl.when(jnp.logical_not(source))
    def _():
        arrived(side, 0, SLICE, 0)
        for yy in (y, 1 - y):
            arrived(across * 2 + yy, 0, HALF, 0)
            arrived(across * 2 + yy, HALF, HALF, 1)

    def second_cols(n, carry):
        col_unpack(n, lambda rows, there: cols[rows, there] + 2.0 * buf[here, rows, there])
        return carry

    lax.fori_loop(0, 4, second_cols, 0)

    def residual(group):
        for i in range(2):
            orbital = group * 2 + i
            for half in range(2):
                rows = pl.ds(pl.multiple_of(orbital * TILE + half * BLK, BLK), BLK)
                here_rows = pl.ds(i * TILE + half * BLK, BLK)
                for p in range(NPB):
                    block = slice(p * BLK, (p + 1) * BLK)
                    value = high[rows, block].astype(F32) + low[rows, block].astype(F32)
                    change = block_of(
                        row_weights, orbital * 2 + half, p, lambda s: buf[group, here_rows, s * BLK : (s + 1) * BLK]
                    )
                    h, l = split(value + 2.0 * change)
                    row_high[half * BLK : (half + 1) * BLK, block] = h
                    row_low[half * BLK : (half + 1) * BLK, block] = l
            rh, rl = row_high[...], row_low[...]
            ch, cl = col_high[...], col_low[...]
            result = dot_nt(rh, ch) + dot_nt(rh, cl) + dot_nt(rl, ch)
            result = -result / ((column_a - occ[orbital]) + row_b)
            for n in range(4):
                place = pl.ds(orbital * (4 * TILE) + n % 2 * 2 + n // 2, TILE, stride=4)
                out[place, :] = result[:, n * BLK : (n + 1) * BLK]

    def wait_chunks(group, sems):
        def one(step, carry):
            for way in range(2):
                ring(group, step, way, sems, va=va).wait_recv()
            return carry

        lax.fori_loop(0, 8, one, 0)

    def phase(n, carry):
        group = jnp.where(n == 0, aux, jnp.where(n == 1, partner, jnp.where(n == 2, far, corner)))

        @pl.when(n == 1)
        def _():
            def onward(step, carry):
                for way in range(2):
                    ring(far, step, way, far_sems, va=va).wait_recv()
                    ring(far, step, way, last_sems, aux=partner).start()
                return carry

            lax.fori_loop(EARLY, 8, onward, 0)
            wait_chunks(partner, pair_sems)

        @pl.when(n == 3)
        def _():
            wait_chunks(corner, last_sems)

        residual(group)
        return carry

    lax.fori_loop(0, 4, phase, 0)

    def ring_drain(step, carry):
        for way in range(2):

            @pl.when(step < 8)
            def _():
                ring(aux, step, way, pair_sems, aux=partner).wait_send()
                ring(far, step, way, last_sems, aux=partner).wait_send()

                @pl.when(source | (step >= EARLY))
                def _():
                    ring(aux, step, way, far_sems, aux=far).wait_send()

            @pl.when(distances[way] < 7)
            def _():
                ref = buf.at[aux, chunk_rows(0, way)]
                put(ref, ref, ring_s.at[way, step], ring_r.at[way, step], vb=up).wait_send()

        return carry

    lax.fori_loop(0, 8 + EARLY, ring_drain, 0)
    lax.fori_loop(0, CHUNKS, spread_drain, 0)
    for copy in sends:
        copy.wait_send()


def body(factors, domains, occ_energy, vir_energy):
    smem = pl.BlockSpec(memory_space=pltpu.SMEM)
    vmem = pl.BlockSpec(memory_space=pltpu.VMEM)
    dma = pltpu.SemaphoreType.DMA
    out = pl.pallas_call(
        kernel,
        out_shape=jax.ShapeDtypeStruct((ROWS * 4, BLK), F32),
        in_specs=[smem, smem, vmem, pl.BlockSpec(memory_space=pl.ANY)],
        out_specs=vmem,
        scratch_shapes=[
            pltpu.VMEM((2, NAUX * O, BLK), F32),
            pltpu.VMEM((ROWS, NAUX), BF16),
            pltpu.VMEM((ROWS, NAUX), BF16),
            pltpu.VMEM((PAIR, PACK), F32),
            pltpu.VMEM((PAIR, NAUX), BF16),
            pltpu.VMEM((PAIR, NAUX), BF16),
            pltpu.VMEM((PAIR, NAUX), F32),
            pltpu.VMEM((PAIR, PACK), F32),
            pltpu.VMEM((5, PAIR, PACK), F32),
            pltpu.VMEM((2, 2, HALF, PACK), F32),
            pltpu.VMEM((2, 2, HALF, PACK), F32),
            pltpu.VMEM((5, SLICE, PACK), F32),
            pltpu.VMEM((TILE, NAUX), BF16),
            pltpu.VMEM((TILE, NAUX), BF16),
            pltpu.SMEM((O * 2 * NPB * 3,), F32),
            pltpu.SMEM((4 * NPB * 3,), F32),
            dma((NPB, 2)), dma((3, CHUNKS, 2)), dma((3, CHUNKS)),
            dma((2, 2)), dma((2, 2)), dma, dma, dma((2, 2)), dma((4,)), dma((2, 2)), dma((4,)),
            dma((5,)), dma((8, 2)), dma((2, 2)),
            dma((2, 8 + EARLY)), dma((2, 8 + EARLY)), dma((2, 8)), dma((2, 8)), dma((2, 8)), dma((2, 8)), dma((2, 8)), dma((2, 8)),
        ],
        compiler_params=pltpu.CompilerParams(collective_id=0, has_side_effects=True, vmem_limit_bytes=VMEM_LIMIT),
        name="amplitudes",
    )(domains.transpose(0, 2, 1), occ_energy, vir_energy.reshape(NVB, BLK), factors.reshape(NAUX * O, TILE))
    return (out * SCALE).reshape(O, TILE, 2, 2, BLK).transpose(0, 1, 3, 2, 4).reshape(O, TILE, 2, TILE)


def solution(mesh):
    placed = (P(None, None, "va"), P(), P(), P())
    return jax.shard_map(
        body, mesh=mesh, in_specs=placed, out_specs=P(None, "va", "aux", "vb"), check_vma=False
    )
```

```python
import math

import jax
import jax.numpy as jnp
from jax import lax
from jax.experimental import pallas as pl
from jax.experimental.pallas import tpu as pltpu
from jax.sharding import PartitionSpec as P

O = 8
V = 2048
NAUX = 1024
BLK = 128
PRESENT = 6
NPB = 8
NVB = 16
TILE = 256
ROWS = O * TILE
PAIR = 2 * TILE
PACK = PRESENT * BLK
SLICE = PAIR // 8
HALF = SLICE // 2
CHUNKS = 8
STEPS = 16
LEAD = 5
QUARTER = SLICE // 4
RING = 16
EARLY = 2
LAG = 2
RING_LAG = 4
SCALE = 8.0 * O * V / math.sqrt(NAUX)
MESH = pl.DeviceIdType.MESH
F32 = jnp.float32
BF16 = jnp.bfloat16
VMEM_LIMIT = 60 * 1024 * 1024

TREES = (
    {0: (1,), 1: (2, 5), 2: (3, 6), 5: (4,), 6: (7,)},
    {0: (3,), 3: (2, 7), 2: (1,), 7: (4, 6), 6: (5,)},
    {0: (4,), 4: (5, 7), 5: (6, 1), 6: (2,), 7: (3,)},
)


def split(value):
    high = value.astype(BF16)
    return high, (value - high.astype(F32)).astype(BF16)


def dot_nt(left, right):
    return lax.dot_general(left, right, (((1,), (1,)), ((), ())), preferred_element_type=F32)


def dot_nn(left, right):
    return lax.dot_general(left, right, (((1,), (0,)), ((), ())), preferred_element_type=F32)


def kernel(
    domains, occ, vir, factors, out,
    raw, high, low, cols, col_high, col_low, total, part, buf, relay, merged, recv, row_high, row_low,
    row_weights, col_weights,
    load, spread_s, spread_r,
    relay_s, relay_r, side_s, side_r, near_s, near_r, merge_s, merge_r,
    ag_s, ag_r, fwd_s, ring_s, ring_r, pair_s, pair_r, far_s, far_r, last_s, last_r,
):
    va, vb, aux = lax.axis_index("va"), lax.axis_index("vb"), lax.axis_index("aux")
    x, y = va // 2, va % 2
    core, hi = aux % 2, aux // 2
    right, left, across = (x + 1) % 4, (x + 3) % 4, (x + 2) % 4
    partner, far, corner = hi * 2 + (1 - core), (aux + 2) % 4, ((1 - hi) * 2) + (1 - core)

    barrier = pltpu.get_barrier_semaphore()
    for k in range(1, 8):
        pl.semaphore_signal(barrier, 1, device_id={"va": (va + k) % 8}, device_id_type=MESH)
    pl.semaphore_signal(barrier, 1, device_id={"vb": (vb + 1) % 8}, device_id_type=MESH)
    pl.semaphore_signal(barrier, 1, device_id={"vb": (vb + 7) % 8}, device_id_type=MESH)
    pl.semaphore_signal(barrier, 1, device_id={"aux": partner}, device_id_type=MESH)
    pl.semaphore_signal(barrier, 1, device_id={"aux": far}, device_id_type=MESH)

    def fetch(p, half):
        rows = pl.ds(p * BLK * O, BLK * O)
        return pltpu.make_async_copy(factors.at[rows, pl.ds(half * BLK, BLK)], raw.at[half, rows], load.at[p, half])

    for p in range(NPB):
        for half in range(2):
            fetch(p, half).start()

    def weigh(table, n, i, block):
        absent = jnp.float32(0)
        for p in range(NPB):
            keep = domains[i, p, block].astype(F32)
            table[(n * NPB + p) * 3] = keep * (1.0 - absent) * (2.0 - absent) * 0.5
            table[(n * NPB + p) * 3 + 1] = keep * absent * (2.0 - absent)
            table[(n * NPB + p) * 3 + 2] = keep * absent * (absent - 1.0) * 0.5
            absent += 1.0 - keep

    def row_tables(n, carry):
        weigh(row_weights, n, n // 2, va * 2 + n % 2)
        return carry

    def col_tables(n, carry):
        weigh(col_weights, n, aux * 2 + n // 2, vb * 2 + n % 2)
        return carry

    lax.fori_loop(0, O * 2, row_tables, 0)
    lax.fori_loop(0, 4, col_tables, 0)

    def slot_of(n, k, full):
        values = [col_weights[(n * NPB + k + d) * 3 + d] * full(k + d) for d in range(3)]
        return values[0] + values[1] + values[2]

    def block_of(table, n, p, slots):
        values = [table[(n * NPB + p) * 3 + d] * slots(p - d) for d in range(3) if 0 <= p - d < PRESENT]
        return sum(values[1:], values[0])

    def lanes(slot):
        return pl.ds(pl.multiple_of(slot * BLK, BLK), BLK)

    def turned(i, half, p):
        keep = domains[i, p, va * 2 + half].astype(F32)
        return raw[half, pl.ds(p * (BLK * O) + i, BLK, stride=O), :].T * keep

    root_x, root_y = vb // 2, vb % 2
    node = (x - root_x + 4) % 4 + 4 * ((y + root_y) % 2)

    for p in range(NPB):
        for half in range(2):
            fetch(p, half).wait()

    @pl.when(node == 0)
    def _():
        def own(n, carry):
            i, half = aux * 2 + n // 2, n % 2
            rows = pl.ds(pl.multiple_of(n * BLK, BLK), BLK)
            for p in range(NPB):
                total[rows, p * BLK : (p + 1) * BLK] = turned(i, half, p)
            for k in range(PRESENT):
                cols[rows, k * BLK : (k + 1) * BLK] = slot_of(n, k, lambda p: total[rows, p * BLK : (p + 1) * BLK])
            return carry

        lax.fori_loop(0, 4, own, 0)

    def lookup(values):
        found = jnp.int32(values[0])
        for n in range(1, 8):
            found = jnp.where(node == n, jnp.int32(values[n]), found)
        return found

    skews, childs = [], []
    for tree in TREES:
        depth = {0: 0}
        todo = [0]
        for n in todo:
            for member in tree.get(n, ()):
                depth[member] = depth[n] + 1
                todo.append(member)
        skews.append(lookup([LEAD + LAG * (depth[n] - 1) for n in range(8)]))
        childs.append([lookup([(*tree.get(n, ()), -1, -1)[k] for n in range(8)]) for k in range(2)])

    def spread(tree, chunk, child, member):
        ref = cols.at[pl.ds(pl.multiple_of(chunk * SLICE, SLICE), SLICE), pl.ds(tree * 256, 256)]
        place = ((root_x + member % 4) % 4) * 2 + (root_y + member // 4) % 2
        return pltpu.make_async_remote_copy(
            ref, ref, spread_s.at[tree, chunk, child], spread_r.at[tree, chunk], device_id={"va": place}, device_id_type=MESH
        )

    pl.semaphore_wait(barrier, 11)

    @pl.when(node == 0)
    def _():
        def launch(chunk, carry):
            for tree in range(3):
                spread(tree, chunk, 0, childs[tree][0]).start()
            return carry

        lax.fori_loop(0, CHUNKS, launch, 0)

    def step(t, carry):
        for tree in range(3):
            chunk = t - skews[tree]

            @pl.when((node != 0) & (chunk >= 0) & (chunk < CHUNKS))
            def _():
                spread(tree, chunk, 0, 0).wait_recv()
                for k in range(2):
                    member = childs[tree][k]

                    @pl.when(member >= 0)
                    def _():
                        spread(tree, chunk, k, member).start()

        @pl.when(t < STEPS)
        def _():
            p = t // 2
            for n in range(4):
                i = (t % 2) * 4 + n
                for half in range(2):
                    h, l = split(turned(i, half, p))
                    rows = pl.ds(pl.multiple_of(i * TILE + half * BLK, BLK), BLK)
                    high[rows, lanes(p)] = h
                    low[rows, lanes(p)] = l

        return carry

    lax.fori_loop(0, LEAD + CHUNKS + 3 * LAG, step, 0)

    def spread_drain(chunk, carry):
        for tree in range(3):
            for k in range(2):
                member = childs[tree][k]

                @pl.when(member >= 0)
                def _():
                    spread(tree, chunk, k, member).wait_send()

        return carry

    def energy_row(tile):
        return [vir[pl.ds(tile * 2 + half, 1), :] for half in range(2)]

    def energy_column(rows):
        return jnp.concatenate([jnp.broadcast_to(row, (8, BLK)).T[:, :1] for row in rows], axis=0)

    rows_a, rows_b = energy_row(va), energy_row(vb)
    row_a = jnp.concatenate(rows_a, axis=1)
    occ_j = [occ[aux * 2 + j] for j in range(2)]
    row_b = jnp.concatenate([row - occ_j[j] for j in range(2) for row in rows_b], axis=1)
    column_a = energy_column(rows_a)
    column_b = energy_column([row - occ_j[j] for j in range(2) for row in rows_b])

    def col_unpack(n, extra):
        rows = pl.ds(pl.multiple_of(n * BLK, BLK), BLK)
        for p in range(NPB):
            h, l = split(block_of(col_weights, n, p, lambda s: extra(rows, slice(s * BLK, (s + 1) * BLK))))
            col_high[rows, p * BLK : (p + 1) * BLK] = h
            col_low[rows, p * BLK : (p + 1) * BLK] = l

    def first_cols(n, carry):
        col_unpack(n, lambda rows, there: cols[rows, there])
        return carry

    lax.fori_loop(0, 4, first_cols, 0)
    total[...] = jnp.zeros_like(total)

    def dress(g, carry):
        ch, cl = col_high[...], col_low[...]
        parts_h, parts_l = [], []
        for i in range(2):
            rows = pl.ds(pl.multiple_of(g * PAIR + i * TILE, TILE), TILE)
            bh, bl = high[rows, :], low[rows, :]
            direct = dot_nt(ch, bh) + dot_nt(ch, bl) + dot_nt(cl, bh)
            energy = column_b + (row_a - occ[g * 2 + i])
            h, l = split(-direct / energy)
            parts_h.append(h)
            parts_l.append(l)
        th, tl = jnp.concatenate(parts_h, axis=1), jnp.concatenate(parts_l, axis=1)
        rows = pl.ds(pl.multiple_of(g * PAIR, PAIR), PAIR)
        bh, bl = high[rows, :], low[rows, :]
        total[...] += dot_nn(th, bh) + dot_nn(th, bl) + dot_nn(tl, bh)
        return carry

    lax.fori_loop(0, 4, dress, 0)

    def pack(n, carry):
        rows = pl.ds(pl.multiple_of(n * BLK, BLK), BLK)
        for k in range(PRESENT):
            part[rows, k * BLK : (k + 1) * BLK] = slot_of(n, k, lambda p: total[rows, p * BLK : (p + 1) * BLK])
        return carry

    lax.fori_loop(0, 4, pack, 0)

    def rows_of(owner, offset, size):
        return pl.ds(pl.multiple_of(owner * SLICE + offset, HALF), size)

    def put(src, dst, s, r, **device):
        return pltpu.make_async_remote_copy(src, dst, s, r, device_id=device, device_id_type=MESH)

    sends = []

    def go(copy):
        copy.start()
        sends.append(copy)

    for yy in range(2):
        opposite = across * 2 + yy
        go(put(part.at[rows_of(opposite, 0, HALF)], relay.at[0, yy], relay_s.at[0, yy], relay_r.at[0, yy], va=right * 2 + y))
        go(put(part.at[rows_of(opposite, HALF, HALF)], relay.at[1, yy], relay_s.at[1, yy], relay_r.at[1, yy], va=left * 2 + y))
    side = x * 2 + 1 - y
    go(put(part.at[rows_of(side, 0, SLICE)], recv.at[4], side_s, side_r, va=side))
    for yy in range(2):
        slot = (yy + y) % 2
        to_right, to_left = right * 2 + yy, left * 2 + yy
        go(put(part.at[rows_of(to_right, HALF, HALF)], recv.at[slot, pl.ds(HALF, HALF)], near_s.at[0, yy], near_r.at[slot], va=to_right))
        go(put(part.at[rows_of(to_left, 0, HALF)], recv.at[2 + slot, pl.ds(0, HALF)], near_s.at[1, yy], near_r.at[2 + slot], va=to_left))
    for yy in range(2):
        slot = (yy + y) % 2
        to_right, to_left = right * 2 + yy, left * 2 + yy
        put(relay.at[0, yy], relay.at[0, yy], relay_s.at[0, yy], relay_r.at[0, yy], va=va).wait_recv()
        merged[0, yy] = part[rows_of(to_right, 0, HALF)] + relay[0, yy]
        go(put(merged.at[0, yy], recv.at[slot, pl.ds(0, HALF)], merge_s.at[0, yy], merge_r.at[slot], va=to_right))
        put(relay.at[1, yy], relay.at[1, yy], relay_s.at[1, yy], relay_r.at[1, yy], va=va).wait_recv()
        merged[1, yy] = part[rows_of(to_left, HALF, HALF)] + relay[1, yy]
        go(put(merged.at[1, yy], recv.at[2 + slot, pl.ds(HALF, HALF)], merge_s.at[1, yy], merge_r.at[2 + slot], va=to_left))
    for slot in range(4):
        put(merged.at[0, 0], recv.at[slot, pl.ds(0, HALF)], near_s.at[0, 0], near_r.at[slot], va=va).wait_recv()
        put(merged.at[0, 0], recv.at[slot, pl.ds(0, HALF)], near_s.at[0, 0], merge_r.at[slot], va=va).wait_recv()
    put(recv.at[4], recv.at[4], side_s, side_r, va=va).wait_recv()

    mine = rows_of(va, 0, SLICE)

    def home(member):
        return jnp.where(member == vb, aux, 4)

    here = home(va)
    buf[here, mine] = part[mine] + ((recv[0] + recv[1]) + (recv[2] + recv[3])) + recv[4]

    def gather(n, target, half):
        rows = rows_of(va, half * HALF, HALF)
        go(put(buf.at[here, rows], buf.at[home(target), rows], ag_s.at[n], ag_r.at[va, half], va=target))

    sides = [m * 2 + yy for yy in (y, 1 - y) for m in (right, left)]
    for n, target in enumerate(sides):
        gather(n, target, n % 2)
    for half in range(2):
        gather(4 + half, side, half)
    for n, target in enumerate(sides):
        gather(6 + n, target, 1 - n % 2)

    def arrived(owner, half):
        ref = buf.at[here, rows_of(owner, half * HALF, HALF)]
        put(ref, ref, side_s, ag_r.at[owner, half], va=va).wait_recv()

    def arrived_rest(n):
        for half in {1: (0, 1), 2: (0,), 3: (0,), 4: (1,), 5: (1,), 6: (0, 1), 7: (0, 1)}[n]:
            arrived(owners[n], half)

    up, down = (vb + 1) % 8, (vb + 7) % 8
    distances = ((vb - va + 8) % 8, (va - vb + 8) % 8)
    owners = (va, side, *(m * 2 + yy for m in (right, left, across) for yy in (y, 1 - y)))

    def chunk_rows(step, way):
        owner = owners[7]
        for n in range(7):
            owner = jnp.where(step // 2 == n, owners[n], owner)
        return pl.ds(pl.multiple_of(owner * SLICE + way * HALF + step % 2 * QUARTER, QUARTER), QUARTER)

    def ring(group, step, way, sems, **device):
        ref = buf.at[group, chunk_rows(step, way)]
        return put(ref, ref, sems[0].at[way, step], sems[1].at[way, step], **device)

    pair_sems, far_sems, last_sems = (pair_s, pair_r), (far_s, far_r), (last_s, last_r)
    lags = [(RING_LAG * d) // 2 for d in distances]
    source = va == vb

    def ring_step(t, carry):
        for way in range(2):
            step = t - lags[way]
            toward = (up, down)[way]

            @pl.when((step >= 0) & (step < RING + EARLY))
            def _():
                late = step >= RING
                local = jnp.where(late, step - RING, step)
                ref = buf.at[jnp.where(late, far, aux), chunk_rows(local, way)]
                along = put(ref, ref, ring_s.at[way, step], ring_r.at[way, step], vb=toward)

                @pl.when(jnp.logical_not(source))
                def _():
                    along.wait_recv()

                @pl.when(source & late)
                def _():
                    ring(far, local, way, far_sems, va=va).wait_recv()

                if way == 0:
                    for n in range(1, 8):

                        @pl.when(source & (step == 2 * n))
                        def _():
                            arrived_rest(n)

                @pl.when(distances[way] < 7)
                def _():
                    along.start()

                @pl.when(jnp.logical_not(late))
                def _():
                    @pl.when(source | (step >= EARLY))
                    def _():
                        ring(aux, local, way, far_sems, aux=far).start()

                    ring(aux, local, way, pair_sems, aux=partner).start()

                @pl.when(late)
                def _():
                    ring(far, local, way, last_sems, aux=partner).start()

        return carry

    @pl.when(source)
    def _():
        ring_step(0, 0)
        ring_step(1, 0)

    for n, yy in enumerate((y, 1 - y)):
        from_left, from_right = left * 2 + yy, right * 2 + yy
        arrived(from_left, 0)
        rows = rows_of(from_left, 0, HALF)
        go(put(buf.at[here, rows], buf.at[home(right * 2 + y), rows], fwd_s.at[0, n], ag_r.at[from_left, 0], va=right * 2 + y))
        arrived(from_right, 1)
        rows = rows_of(from_right, HALF, HALF)
        go(put(buf.at[here, rows], buf.at[home(left * 2 + y), rows], fwd_s.at[1, n], ag_r.at[from_right, 1], va=left * 2 + y))

    lax.fori_loop(2, RING + EARLY + (RING_LAG * 7) // 2, ring_step, 0)

    @pl.when(jnp.logical_not(source))
    def _():
        for n in range(1, 8):
            arrived_rest(n)

    def second_cols(n, carry):
        col_unpack(n, lambda rows, there: cols[rows, there] + 2.0 * buf[here, rows, there])
        return carry

    lax.fori_loop(0, 4, second_cols, 0)

    def residual(group):
        for i in range(2):
            orbital = group * 2 + i
            for half in range(2):
                rows = pl.ds(pl.multiple_of(orbital * TILE + half * BLK, BLK), BLK)
                here_rows = pl.ds(i * TILE + half * BLK, BLK)
                for p in range(NPB):
                    block = slice(p * BLK, (p + 1) * BLK)
                    value = high[rows, block].astype(F32) + low[rows, block].astype(F32)
                    change = block_of(
                        row_weights, orbital * 2 + half, p, lambda s: buf[group, here_rows, s * BLK : (s + 1) * BLK]
                    )
                    h, l = split(value + 2.0 * change)
                    row_high[half * BLK : (half + 1) * BLK, block] = h
                    row_low[half * BLK : (half + 1) * BLK, block] = l
            rh, rl = row_high[...], row_low[...]
            ch, cl = col_high[...], col_low[...]
            result = dot_nt(rh, ch) + dot_nt(rh, cl) + dot_nt(rl, ch)
            result = -result / ((column_a - occ[orbital]) + row_b)
            for n in range(4):
                place = pl.ds(orbital * (4 * TILE) + n % 2 * 2 + n // 2, TILE, stride=4)
                out[place, :] = result[:, n * BLK : (n + 1) * BLK]

    def wait_chunks(group, sems):
        def one(step, carry):
            for way in range(2):
                ring(group, step, way, sems, va=va).wait_recv()
            return carry

        lax.fori_loop(0, RING, one, 0)

    def phase(n, carry):
        group = jnp.where(n == 0, aux, jnp.where(n == 1, partner, jnp.where(n == 2, far, corner)))

        @pl.when(n == 1)
        def _():
            def onward(step, carry):
                for way in range(2):
                    ring(far, step, way, far_sems, va=va).wait_recv()
                    ring(far, step, way, last_sems, aux=partner).start()
                return carry

            lax.fori_loop(EARLY, RING, onward, 0)
            wait_chunks(partner, pair_sems)

        @pl.when(n == 3)
        def _():
            wait_chunks(corner, last_sems)

        residual(group)
        return carry

    lax.fori_loop(0, 4, phase, 0)

    def ring_drain(step, carry):
        for way in range(2):

            @pl.when(step < RING)
            def _():
                ring(aux, step, way, pair_sems, aux=partner).wait_send()
                ring(far, step, way, last_sems, aux=partner).wait_send()

                @pl.when(source | (step >= EARLY))
                def _():
                    ring(aux, step, way, far_sems, aux=far).wait_send()

            @pl.when(distances[way] < 7)
            def _():
                ref = buf.at[aux, chunk_rows(0, way)]
                put(ref, ref, ring_s.at[way, step], ring_r.at[way, step], vb=up).wait_send()

        return carry

    lax.fori_loop(0, RING + EARLY, ring_drain, 0)
    lax.fori_loop(0, CHUNKS, spread_drain, 0)
    for copy in sends:
        copy.wait_send()


def body(factors, domains, occ_energy, vir_energy):
    smem = pl.BlockSpec(memory_space=pltpu.SMEM)
    vmem = pl.BlockSpec(memory_space=pltpu.VMEM)
    dma = pltpu.SemaphoreType.DMA
    out = pl.pallas_call(
        kernel,
        out_shape=jax.ShapeDtypeStruct((ROWS * 4, BLK), F32),
        in_specs=[smem, smem, vmem, pl.BlockSpec(memory_space=pl.ANY)],
        out_specs=vmem,
        scratch_shapes=[
            pltpu.VMEM((2, NAUX * O, BLK), F32),
            pltpu.VMEM((ROWS, NAUX), BF16),
            pltpu.VMEM((ROWS, NAUX), BF16),
            pltpu.VMEM((PAIR, PACK), F32),
            pltpu.VMEM((PAIR, NAUX), BF16),
            pltpu.VMEM((PAIR, NAUX), BF16),
            pltpu.VMEM((PAIR, NAUX), F32),
            pltpu.VMEM((PAIR, PACK), F32),
            pltpu.VMEM((5, PAIR, PACK), F32),
            pltpu.VMEM((2, 2, HALF, PACK), F32),
            pltpu.VMEM((2, 2, HALF, PACK), F32),
            pltpu.VMEM((5, SLICE, PACK), F32),
            pltpu.VMEM((TILE, NAUX), BF16),
            pltpu.VMEM((TILE, NAUX), BF16),
            pltpu.SMEM((O * 2 * NPB * 3,), F32),
            pltpu.SMEM((4 * NPB * 3,), F32),
            dma((NPB, 2)), dma((3, CHUNKS, 2)), dma((3, CHUNKS)),
            dma((2, 2)), dma((2, 2)), dma, dma, dma((2, 2)), dma((4,)), dma((2, 2)), dma((4,)),
            dma((10,)), dma((8, 2)), dma((2, 2)),
            dma((2, RING + EARLY)), dma((2, RING + EARLY)), dma((2, RING)), dma((2, RING)), dma((2, RING)), dma((2, RING)), dma((2, RING)), dma((2, RING)),
        ],
        compiler_params=pltpu.CompilerParams(collective_id=0, has_side_effects=True, vmem_limit_bytes=VMEM_LIMIT),
        name="amplitudes",
    )(domains.transpose(0, 2, 1), occ_energy, vir_energy.reshape(NVB, BLK), factors.reshape(NAUX * O, TILE))
    return (out * SCALE).reshape(O, TILE, 2, 2, BLK).transpose(0, 1, 3, 2, 4).reshape(O, TILE, 2, TILE)


def solution(mesh):
    placed = (P(None, None, "va"), P(), P(), P())
    return jax.shard_map(
        body, mesh=mesh, in_specs=placed, out_specs=P(None, "va", "aux", "vb"), check_vma=False
    )
```

```python
import math

import jax
import jax.numpy as jnp
from jax import lax
from jax.experimental import pallas as pl
from jax.experimental.pallas import tpu as pltpu
from jax.sharding import PartitionSpec as P

O = 8
V = 2048
NAUX = 1024
BLK = 128
PRESENT = 6
NPB = 8
NVB = 16
TILE = 256
ROWS = O * TILE
PAIR = 2 * TILE
PACK = PRESENT * BLK
SLICE = PAIR // 8
HALF = SLICE // 2
CHUNKS = 8
STEPS = 16
LEAD = 5
RING = 8
EARLY = 1
ORDER = (4, 3, 5, 2, 6, 1, 7)
LAG = 2
RING_LAG = 4
SCALE = 8.0 * O * V / math.sqrt(NAUX)
MESH = pl.DeviceIdType.MESH
F32 = jnp.float32
BF16 = jnp.bfloat16
VMEM_LIMIT = 60 * 1024 * 1024

TREES = (
    {0: (1,), 1: (2, 5), 2: (3, 6), 5: (4,), 6: (7,)},
    {0: (3,), 3: (2, 7), 2: (1,), 7: (4, 6), 6: (5,)},
    {0: (4,), 4: (5, 7), 5: (6, 1), 6: (2,), 7: (3,)},
)


def split(value):
    high = value.astype(BF16)
    return high, (value - high.astype(F32)).astype(BF16)


def dot_nt(left, right):
    return lax.dot_general(left, right, (((1,), (1,)), ((), ())), preferred_element_type=F32)


def dot_nn(left, right):
    return lax.dot_general(left, right, (((1,), (0,)), ((), ())), preferred_element_type=F32)


def kernel(
    domains, occ, vir, factors, out,
    raw, high, low, cols, col_high, col_low, total, part, buf, recv, row_high, row_low,
    row_weights, col_weights,
    load, spread_s, spread_r,
    rs_s, rs_r, ag_s, ag_r, ring_s, ring_r, pair_s, pair_r, far_s, far_r, last_s, last_r,
):
    va, vb, aux = lax.axis_index("va"), lax.axis_index("vb"), lax.axis_index("aux")
    x, y = va // 2, va % 2
    core, hi = aux % 2, aux // 2
    right, left, across = (x + 1) % 4, (x + 3) % 4, (x + 2) % 4
    partner, far, corner = hi * 2 + (1 - core), (aux + 2) % 4, ((1 - hi) * 2) + (1 - core)

    barrier = pltpu.get_barrier_semaphore()
    for k in range(1, 8):
        pl.semaphore_signal(barrier, 1, device_id={"va": (va + k) % 8}, device_id_type=MESH)
    pl.semaphore_signal(barrier, 1, device_id={"vb": (vb + 1) % 8}, device_id_type=MESH)
    pl.semaphore_signal(barrier, 1, device_id={"vb": (vb + 7) % 8}, device_id_type=MESH)
    pl.semaphore_signal(barrier, 1, device_id={"aux": partner}, device_id_type=MESH)
    pl.semaphore_signal(barrier, 1, device_id={"aux": far}, device_id_type=MESH)

    def fetch(p, half):
        rows = pl.ds(p * BLK * O, BLK * O)
        return pltpu.make_async_copy(factors.at[rows, pl.ds(half * BLK, BLK)], raw.at[half, rows], load.at[p, half])

    for p in range(NPB):
        for half in range(2):
            fetch(p, half).start()

    def weigh(table, n, i, block):
        absent = jnp.float32(0)
        for p in range(NPB):
            keep = domains[i, p, block].astype(F32)
            table[(n * NPB + p) * 3] = keep * (1.0 - absent) * (2.0 - absent) * 0.5
            table[(n * NPB + p) * 3 + 1] = keep * absent * (2.0 - absent)
            table[(n * NPB + p) * 3 + 2] = keep * absent * (absent - 1.0) * 0.5
            absent += 1.0 - keep

    def row_tables(n, carry):
        weigh(row_weights, n, n // 2, va * 2 + n % 2)
        return carry

    def col_tables(n, carry):
        weigh(col_weights, n, aux * 2 + n // 2, vb * 2 + n % 2)
        return carry

    lax.fori_loop(0, O * 2, row_tables, 0)
    lax.fori_loop(0, 4, col_tables, 0)

    def slot_of(n, k, full):
        values = [col_weights[(n * NPB + k + d) * 3 + d] * full(k + d) for d in range(3)]
        return values[0] + values[1] + values[2]

    def block_of(table, n, p, slots):
        values = [table[(n * NPB + p) * 3 + d] * slots(p - d) for d in range(3) if 0 <= p - d < PRESENT]
        return sum(values[1:], values[0])

    def lanes(slot):
        return pl.ds(pl.multiple_of(slot * BLK, BLK), BLK)

    def turned(i, half, p):
        keep = domains[i, p, va * 2 + half].astype(F32)
        return raw[half, pl.ds(p * (BLK * O) + i, BLK, stride=O), :].T * keep

    root_x, root_y = vb // 2, vb % 2
    node = (x - root_x + 4) % 4 + 4 * ((y + root_y) % 2)

    for p in range(NPB):
        for half in range(2):
            fetch(p, half).wait()

    @pl.when(node == 0)
    def _():
        def own(n, carry):
            i, half = aux * 2 + n // 2, n % 2
            rows = pl.ds(pl.multiple_of(n * BLK, BLK), BLK)
            for p in range(NPB):
                total[rows, p * BLK : (p + 1) * BLK] = turned(i, half, p)
            for k in range(PRESENT):
                cols[rows, k * BLK : (k + 1) * BLK] = slot_of(n, k, lambda p: total[rows, p * BLK : (p + 1) * BLK])
            return carry

        lax.fori_loop(0, 4, own, 0)

    def lookup(values):
        found = jnp.int32(values[0])
        for n in range(1, 8):
            found = jnp.where(node == n, jnp.int32(values[n]), found)
        return found

    skews, childs = [], []
    for tree in TREES:
        depth = {0: 0}
        todo = [0]
        for n in todo:
            for member in tree.get(n, ()):
                depth[member] = depth[n] + 1
                todo.append(member)
        skews.append(lookup([LEAD + LAG * (depth[n] - 1) for n in range(8)]))
        childs.append([lookup([(*tree.get(n, ()), -1, -1)[k] for n in range(8)]) for k in range(2)])

    def spread(tree, chunk, child, member):
        ref = cols.at[pl.ds(pl.multiple_of(chunk * SLICE, SLICE), SLICE), pl.ds(tree * 256, 256)]
        place = ((root_x + member % 4) % 4) * 2 + (root_y + member // 4) % 2
        return pltpu.make_async_remote_copy(
            ref, ref, spread_s.at[tree, chunk, child], spread_r.at[tree, chunk], device_id={"va": place}, device_id_type=MESH
        )

    pl.semaphore_wait(barrier, 11)

    @pl.when(node == 0)
    def _():
        def launch(chunk, carry):
            for tree in range(3):
                spread(tree, chunk, 0, childs[tree][0]).start()
            return carry

        lax.fori_loop(0, CHUNKS, launch, 0)

    def relay(t):
        for tree in range(3):
            chunk = t - skews[tree]

            @pl.when((node != 0) & (chunk >= 0) & (chunk < CHUNKS))
            def _():
                spread(tree, chunk, 0, 0).wait_recv()
                for k in range(2):
                    member = childs[tree][k]

                    @pl.when(member >= 0)
                    def _():
                        spread(tree, chunk, k, member).start()

    def prepare(t, carry):
        relay(t)
        p = t // 2
        for n in range(4):
            i = (t % 2) * 4 + n
            for half in range(2):
                h, l = split(turned(i, half, p))
                rows = pl.ds(pl.multiple_of(i * TILE + half * BLK, BLK), BLK)
                high[rows, lanes(p)] = h
                low[rows, lanes(p)] = l
        return carry

    lax.fori_loop(0, STEPS, prepare, 0)

    def spread_drain(chunk, carry):
        for tree in range(3):
            for k in range(2):
                member = childs[tree][k]

                @pl.when(member >= 0)
                def _():
                    spread(tree, chunk, k, member).wait_send()

        return carry

    def energy_row(tile):
        return [vir[pl.ds(tile * 2 + half, 1), :] for half in range(2)]

    def energy_column(rows):
        return jnp.concatenate([jnp.broadcast_to(row, (8, BLK)).T[:, :1] for row in rows], axis=0)

    rows_a, rows_b = energy_row(va), energy_row(vb)
    row_a = jnp.concatenate(rows_a, axis=1)
    occ_j = [occ[aux * 2 + j] for j in range(2)]
    row_b = jnp.concatenate([row - occ_j[j] for j in range(2) for row in rows_b], axis=1)
    column_a = energy_column(rows_a)
    column_b = energy_column([row - occ_j[j] for j in range(2) for row in rows_b])

    def col_unpack(n, extra):
        rows = pl.ds(pl.multiple_of(n * BLK, BLK), BLK)
        for p in range(NPB):
            h, l = split(block_of(col_weights, n, p, lambda s: extra(rows, slice(s * BLK, (s + 1) * BLK))))
            col_high[rows, p * BLK : (p + 1) * BLK] = h
            col_low[rows, p * BLK : (p + 1) * BLK] = l

    def first_cols(n, carry):
        col_unpack(n, lambda rows, there: cols[rows, there])
        return carry

    def dress(j):
        mine = slice(j * TILE, (j + 1) * TILE)

        def one(g, carry):
            if j == 0:
                relay(STEPS + g)
            ch, cl = col_high[mine, :], col_low[mine, :]
            parts_h, parts_l = [], []
            for i in range(2):
                rows = pl.ds(pl.multiple_of(g * PAIR + i * TILE, TILE), TILE)
                bh, bl = high[rows, :], low[rows, :]
                direct = dot_nt(ch, bh) + dot_nt(ch, bl) + dot_nt(cl, bh)
                energy = column_b[mine, :] + (row_a - occ[g * 2 + i])
                h, l = split(-direct / energy)
                parts_h.append(h)
                parts_l.append(l)
            th, tl = jnp.concatenate(parts_h, axis=1), jnp.concatenate(parts_l, axis=1)
            rows = pl.ds(pl.multiple_of(g * PAIR, PAIR), PAIR)
            bh, bl = high[rows, :], low[rows, :]
            total[mine, :] += dot_nn(th, bh) + dot_nn(th, bl) + dot_nn(tl, bh)
            return carry

        lax.fori_loop(2 * j, 2 * j + 2, first_cols, 0)
        total[mine, :] = jnp.zeros((TILE, NAUX), F32)
        lax.fori_loop(0, 4, one, 0)

    def pack(n, carry):
        rows = pl.ds(pl.multiple_of(n * BLK, BLK), BLK)
        for k in range(PRESENT):
            part[rows, k * BLK : (k + 1) * BLK] = slot_of(n, k, lambda p: total[rows, p * BLK : (p + 1) * BLK])
        return carry

    def put(src, dst, s, r, **device):
        return pltpu.make_async_remote_copy(src, dst, s, r, device_id=device, device_id_type=MESH)

    def piece(j, owner):
        return pl.ds(pl.multiple_of(j * TILE + owner * HALF, HALF), HALF)

    def home(member):
        return jnp.where(member == vb, aux, 4)

    here = home(va)
    sends = []

    def scatter(j):
        lax.fori_loop(2 * j, 2 * j + 2, pack, 0)
        for k in ORDER:
            target = (va + k) % 8
            copy = put(part.at[piece(j, target)], recv.at[j, k - 1], rs_s.at[j, k - 1], rs_r.at[j, k - 1], va=target)
            copy.start()
            sends.append(copy)

    def gather(j):
        for k in range(7):
            put(recv.at[j, k], recv.at[j, k], rs_s.at[j, k], rs_r.at[j, k], va=va).wait_recv()
        rows = piece(j, va)
        value = ((recv[j, 0] + recv[j, 1]) + (recv[j, 2] + recv[j, 3])) + ((recv[j, 4] + recv[j, 5]) + recv[j, 6])
        buf[here, rows] = part[rows] + value
        for k in ORDER:
            target = (va + k) % 8
            copy = put(buf.at[here, rows], buf.at[home(target), rows], ag_s.at[j, k - 1], ag_r.at[j, va], va=target)
            copy.start()
            sends.append(copy)

    def gathered(j, owner):
        ref = buf.at[here, piece(j, owner)]
        put(ref, ref, ag_s.at[j, 0], ag_r.at[j, owner], va=va).wait_recv()

    dress(0)
    scatter(0)
    dress(1)
    scatter(1)
    gather(0)

    up, down = (vb + 1) % 8, (vb + 7) % 8
    distances = ((vb - va + 8) % 8, (va - vb + 8) % 8)
    owners = (va, x * 2 + 1 - y, *(m * 2 + yy for yy in (y, 1 - y) for m in (right, left)), across * 2 + y, across * 2 + 1 - y)

    def owner_of(step, way):
        owner = owners[6 + way]
        for n in range(3):
            owner = jnp.where(step % 4 == n, owners[2 * n + way], owner)
        return owner

    def chunk_rows(step, way):
        return piece(step // 4, owner_of(step, way))

    def ring(group, step, way, sems, **device):
        ref = buf.at[group, chunk_rows(step, way)]
        return put(ref, ref, sems[0].at[way, step], sems[1].at[way, step], **device)

    pair_sems, far_sems, last_sems = (pair_s, pair_r), (far_s, far_r), (last_s, last_r)
    lags = [(RING_LAG * d) // 2 for d in distances]
    source = va == vb

    def ring_step(t, carry):
        for way in range(2):
            step = t - lags[way]
            toward = (up, down)[way]

            @pl.when((step >= 0) & (step < RING + EARLY))
            def _():
                late = step >= RING
                local = jnp.where(late, step - RING, step)
                ref = buf.at[jnp.where(late, far, aux), chunk_rows(local, way)]
                along = put(ref, ref, ring_s.at[way, step], ring_r.at[way, step], vb=toward)

                @pl.when(jnp.logical_not(source))
                def _():
                    along.wait_recv()

                @pl.when(source & late)
                def _():
                    ring(far, local, way, far_sems, va=va).wait_recv()

                @pl.when(source & jnp.logical_not(late) & ((step % 4 != 0) | (way != 0)))
                def _():
                    gathered(local // 4, owner_of(local, way))

                @pl.when(distances[way] < 7)
                def _():
                    along.start()

                @pl.when(jnp.logical_not(late))
                def _():
                    @pl.when(source | (step >= EARLY))
                    def _():
                        ring(aux, local, way, far_sems, aux=far).start()

                    ring(aux, local, way, pair_sems, aux=partner).start()

                @pl.when(late)
                def _():
                    ring(far, local, way, last_sems, aux=partner).start()

        return carry

    @pl.when(source)
    def _():
        ring_step(0, 0)

    gather(1)
    lax.fori_loop(1, RING + EARLY + (RING_LAG * 7) // 2, ring_step, 0)

    @pl.when(jnp.logical_not(source))
    def _():
        for j in range(2):
            for owner in owners[1:]:
                gathered(j, owner)

    def second_cols(n, carry):
        col_unpack(n, lambda rows, there: cols[rows, there] + 2.0 * buf[here, rows, there])
        return carry

    lax.fori_loop(0, 4, second_cols, 0)

    def residual(group):
        for i in range(2):
            orbital = group * 2 + i
            for half in range(2):
                rows = pl.ds(pl.multiple_of(orbital * TILE + half * BLK, BLK), BLK)
                here_rows = pl.ds(i * TILE + half * BLK, BLK)
                for p in range(NPB):
                    block = slice(p * BLK, (p + 1) * BLK)
                    value = high[rows, block].astype(F32) + low[rows, block].astype(F32)
                    change = block_of(
                        row_weights, orbital * 2 + half, p, lambda s: buf[group, here_rows, s * BLK : (s + 1) * BLK]
                    )
                    h, l = split(value + 2.0 * change)
                    row_high[half * BLK : (half + 1) * BLK, block] = h
                    row_low[half * BLK : (half + 1) * BLK, block] = l
            rh, rl = row_high[...], row_low[...]
            ch, cl = col_high[...], col_low[...]
            result = dot_nt(rh, ch) + dot_nt(rh, cl) + dot_nt(rl, ch)
            result = -result / ((column_a - occ[orbital]) + row_b)
            for n in range(4):
                place = pl.ds(orbital * (4 * TILE) + n % 2 * 2 + n // 2, TILE, stride=4)
                out[place, :] = result[:, n * BLK : (n + 1) * BLK]

    def wait_chunks(group, sems):
        def one(step, carry):
            for way in range(2):
                ring(group, step, way, sems, va=va).wait_recv()
            return carry

        lax.fori_loop(0, RING, one, 0)

    def phase(n, carry):
        group = jnp.where(n == 0, aux, jnp.where(n == 1, partner, jnp.where(n == 2, far, corner)))

        @pl.when(n == 1)
        def _():
            def onward(step, carry):
                for way in range(2):
                    ring(far, step, way, far_sems, va=va).wait_recv()
                    ring(far, step, way, last_sems, aux=partner).start()
                return carry

            lax.fori_loop(EARLY, RING, onward, 0)
            wait_chunks(partner, pair_sems)

        @pl.when(n == 3)
        def _():
            wait_chunks(corner, last_sems)

        residual(group)
        return carry

    lax.fori_loop(0, 4, phase, 0)

    def ring_drain(step, carry):
        for way in range(2):

            @pl.when(step < RING)
            def _():
                ring(aux, step, way, pair_sems, aux=partner).wait_send()
                ring(far, step, way, last_sems, aux=partner).wait_send()

                @pl.when(source | (step >= EARLY))
                def _():
                    ring(aux, step, way, far_sems, aux=far).wait_send()

            @pl.when(distances[way] < 7)
            def _():
                ref = buf.at[aux, chunk_rows(0, way)]
                put(ref, ref, ring_s.at[way, step], ring_r.at[way, step], vb=up).wait_send()

        return carry

    lax.fori_loop(0, RING + EARLY, ring_drain, 0)
    lax.fori_loop(0, CHUNKS, spread_drain, 0)
    for copy in sends:
        copy.wait_send()


def body(factors, domains, occ_energy, vir_energy):
    smem = pl.BlockSpec(memory_space=pltpu.SMEM)
    vmem = pl.BlockSpec(memory_space=pltpu.VMEM)
    dma = pltpu.SemaphoreType.DMA
    out = pl.pallas_call(
        kernel,
        out_shape=jax.ShapeDtypeStruct((ROWS * 4, BLK), F32),
        in_specs=[smem, smem, vmem, pl.BlockSpec(memory_space=pltpu.HBM)],
        out_specs=vmem,
        scratch_shapes=[
            pltpu.VMEM((2, NAUX * O, BLK), F32),
            pltpu.VMEM((ROWS, NAUX), BF16),
            pltpu.VMEM((ROWS, NAUX), BF16),
            pltpu.VMEM((PAIR, PACK), F32),
            pltpu.VMEM((PAIR, NAUX), BF16),
            pltpu.VMEM((PAIR, NAUX), BF16),
            pltpu.VMEM((PAIR, NAUX), F32),
            pltpu.VMEM((PAIR, PACK), F32),
            pltpu.VMEM((5, PAIR, PACK), F32),
            pltpu.VMEM((2, 7, HALF, PACK), F32),
            pltpu.VMEM((TILE, NAUX), BF16),
            pltpu.VMEM((TILE, NAUX), BF16),
            pltpu.SMEM((O * 2 * NPB * 3,), F32),
            pltpu.SMEM((4 * NPB * 3,), F32),
            dma((NPB, 2)), dma((3, CHUNKS, 2)), dma((3, CHUNKS)),
            dma((2, 7)), dma((2, 7)), dma((2, 7)), dma((2, 8)),
            dma((2, RING + EARLY)), dma((2, RING + EARLY)), dma((2, RING)), dma((2, RING)), dma((2, RING)), dma((2, RING)), dma((2, RING)), dma((2, RING)),
        ],
        compiler_params=pltpu.CompilerParams(collective_id=0, has_side_effects=True, vmem_limit_bytes=VMEM_LIMIT),
        name="amplitudes",
    )(domains.transpose(0, 2, 1), occ_energy, vir_energy.reshape(NVB, BLK), factors.reshape(NAUX * O, TILE))
    return (out * SCALE).reshape(O, TILE, 2, 2, BLK).transpose(0, 1, 3, 2, 4).reshape(O, TILE, 2, TILE)


def solution(mesh):
    placed = (P(None, None, "va"), P(), P(), P())
    return jax.shard_map(
        body, mesh=mesh, in_specs=placed, out_specs=P(None, "va", "aux", "vb"), check_vma=False
    )
```

```python
import math

import jax
import jax.numpy as jnp
from jax import lax
from jax.experimental import pallas as pl
from jax.experimental.pallas import tpu as pltpu
from jax.sharding import PartitionSpec as P

O = 8
V = 2048
NAUX = 1024
BLK = 128
PRESENT = 6
NPB = 8
NVB = 16
TILE = 256
ROWS = O * TILE
PAIR = 2 * TILE
PACK = PRESENT * BLK
SLICE = PAIR // 8
HALF = SLICE // 2
CHUNKS = 8
STEPS = 16
LEAD = 5
RING = 8
EARLY = 1
ORDER = (4, 3, 5, 2, 6, 1, 7)
LAG = 2
RING_LAG = 4
SCALE = 8.0 * O * V / math.sqrt(NAUX)
MESH = pl.DeviceIdType.MESH
F32 = jnp.float32
BF16 = jnp.bfloat16
VMEM_LIMIT = 60 * 1024 * 1024

TREES = (
    {0: (1,), 1: (2, 5), 2: (3, 6), 5: (4,), 6: (7,)},
    {0: (3,), 3: (2, 7), 2: (1,), 7: (4, 6), 6: (5,)},
    {0: (4,), 4: (5, 7), 5: (6, 1), 6: (2,), 7: (3,)},
)


def split(value):
    high = value.astype(BF16)
    return high, (value - high.astype(F32)).astype(BF16)


def dot_nt(left, right):
    return lax.dot_general(left, right, (((1,), (1,)), ((), ())), preferred_element_type=F32)


def dot_nn(left, right):
    return lax.dot_general(left, right, (((1,), (0,)), ((), ())), preferred_element_type=F32)


def kernel(
    domains, occ, vir, factors, out,
    raw, high, low, cols, col_high, col_low, total, part, buf, recv, row_high, row_low,
    row_weights, col_weights,
    load, spread_s, spread_r,
    rs_s, rs_r, ag_s, ag_r, ring_s, ring_r, pair_s, pair_r, far_s, far_r, last_s, last_r,
):
    va, vb, aux = lax.axis_index("va"), lax.axis_index("vb"), lax.axis_index("aux")
    x, y = va // 2, va % 2
    core, hi = aux % 2, aux // 2
    right, left, across = (x + 1) % 4, (x + 3) % 4, (x + 2) % 4
    partner, far, corner = hi * 2 + (1 - core), (aux + 2) % 4, ((1 - hi) * 2) + (1 - core)

    barrier = pltpu.get_barrier_semaphore()
    for k in range(1, 8):
        pl.semaphore_signal(barrier, 1, device_id={"va": (va + k) % 8}, device_id_type=MESH)
    pl.semaphore_signal(barrier, 1, device_id={"vb": (vb + 1) % 8}, device_id_type=MESH)
    pl.semaphore_signal(barrier, 1, device_id={"vb": (vb + 7) % 8}, device_id_type=MESH)
    pl.semaphore_signal(barrier, 1, device_id={"aux": partner}, device_id_type=MESH)
    pl.semaphore_signal(barrier, 1, device_id={"aux": far}, device_id_type=MESH)

    def fetch(p, half):
        rows = pl.ds(p * BLK * O, BLK * O)
        return pltpu.make_async_copy(factors.at[rows, pl.ds(half * BLK, BLK)], raw.at[half, rows], load.at[p, half])

    for p in range(NPB):
        for half in range(2):
            fetch(p, half).start()

    def weigh(table, n, i, block):
        absent = jnp.float32(0)
        for p in range(NPB):
            keep = domains[i, p, block].astype(F32)
            table[(n * NPB + p) * 3] = keep * (1.0 - absent) * (2.0 - absent) * 0.5
            table[(n * NPB + p) * 3 + 1] = keep * absent * (2.0 - absent)
            table[(n * NPB + p) * 3 + 2] = keep * absent * (absent - 1.0) * 0.5
            absent += 1.0 - keep

    def row_tables(n, carry):
        weigh(row_weights, n, n // 2, va * 2 + n % 2)
        return carry

    def col_tables(n, carry):
        weigh(col_weights, n, aux * 2 + n // 2, vb * 2 + n % 2)
        return carry

    lax.fori_loop(0, O * 2, row_tables, 0)
    lax.fori_loop(0, 4, col_tables, 0)

    def slot_of(n, k, full):
        values = [col_weights[(n * NPB + k + d) * 3 + d] * full(k + d) for d in range(3)]
        return values[0] + values[1] + values[2]

    def block_of(table, n, p, slots):
        values = [table[(n * NPB + p) * 3 + d] * slots(p - d) for d in range(3) if 0 <= p - d < PRESENT]
        return sum(values[1:], values[0])

    def lanes(slot):
        return pl.ds(pl.multiple_of(slot * BLK, BLK), BLK)

    def turned(i, half, p):
        keep = domains[i, p, va * 2 + half].astype(F32)
        return raw[half, pl.ds(p * (BLK * O) + i, BLK, stride=O), :].T * keep

    root_x, root_y = vb // 2, vb % 2
    node = (x - root_x + 4) % 4 + 4 * ((y + root_y) % 2)

    for p in range(NPB):
        for half in range(2):
            fetch(p, half).wait()

    @pl.when(node == 0)
    def _():
        def own(n, carry):
            i, half = aux * 2 + n // 2, n % 2
            rows = pl.ds(pl.multiple_of(n * BLK, BLK), BLK)
            for p in range(NPB):
                total[rows, p * BLK : (p + 1) * BLK] = turned(i, half, p)
            for k in range(PRESENT):
                cols[rows, k * BLK : (k + 1) * BLK] = slot_of(n, k, lambda p: total[rows, p * BLK : (p + 1) * BLK])
            return carry

        lax.fori_loop(0, 4, own, 0)

    def lookup(values):
        found = jnp.int32(values[0])
        for n in range(1, 8):
            found = jnp.where(node == n, jnp.int32(values[n]), found)
        return found

    skews, childs = [], []
    for tree in TREES:
        depth = {0: 0}
        todo = [0]
        for n in todo:
            for member in tree.get(n, ()):
                depth[member] = depth[n] + 1
                todo.append(member)
        skews.append(lookup([LEAD + LAG * (depth[n] - 1) for n in range(8)]))
        childs.append([lookup([(*tree.get(n, ()), -1, -1)[k] for n in range(8)]) for k in range(2)])

    def spread(tree, chunk, child, member):
        ref = cols.at[pl.ds(pl.multiple_of(chunk * SLICE, SLICE), SLICE), pl.ds(tree * 256, 256)]
        place = ((root_x + member % 4) % 4) * 2 + (root_y + member // 4) % 2
        return pltpu.make_async_remote_copy(
            ref, ref, spread_s.at[tree, chunk, child], spread_r.at[tree, chunk], device_id={"va": place}, device_id_type=MESH
        )

    pl.semaphore_wait(barrier, 11)

    @pl.when(node == 0)
    def _():
        def launch(chunk, carry):
            for tree in range(3):
                spread(tree, chunk, 0, childs[tree][0]).start()
            return carry

        lax.fori_loop(0, CHUNKS, launch, 0)

    def relay(t):
        for tree in range(3):
            chunk = t - skews[tree]

            @pl.when((node != 0) & (chunk >= 0) & (chunk < CHUNKS))
            def _():
                spread(tree, chunk, 0, 0).wait_recv()
                for k in range(2):
                    member = childs[tree][k]

                    @pl.when(member >= 0)
                    def _():
                        spread(tree, chunk, k, member).start()

    def prepare(t, carry):
        relay(t)
        p = t // 2
        for n in range(4):
            i = (t % 2) * 4 + n
            for half in range(2):
                h, l = split(turned(i, half, p))
                rows = pl.ds(pl.multiple_of(i * TILE + half * BLK, BLK), BLK)
                high[rows, lanes(p)] = h
                low[rows, lanes(p)] = l
        return carry

    lax.fori_loop(0, STEPS, prepare, 0)

    def spread_drain(chunk, carry):
        for tree in range(3):
            for k in range(2):
                member = childs[tree][k]

                @pl.when(member >= 0)
                def _():
                    spread(tree, chunk, k, member).wait_send()

        return carry

    def energy_row(tile):
        return [vir[pl.ds(tile * 2 + half, 1), :] for half in range(2)]

    def energy_column(rows):
        return jnp.concatenate([jnp.broadcast_to(row, (8, BLK)).T[:, :1] for row in rows], axis=0)

    rows_a, rows_b = energy_row(va), energy_row(vb)
    row_a = jnp.concatenate(rows_a, axis=1)
    occ_j = [occ[aux * 2 + j] for j in range(2)]
    row_b = jnp.concatenate([row - occ_j[j] for j in range(2) for row in rows_b], axis=1)
    column_a = energy_column(rows_a)
    column_b = energy_column([row - occ_j[j] for j in range(2) for row in rows_b])

    def col_unpack(n, extra):
        rows = pl.ds(pl.multiple_of(n * BLK, BLK), BLK)
        for p in range(NPB):
            h, l = split(block_of(col_weights, n, p, lambda s: extra(rows, slice(s * BLK, (s + 1) * BLK))))
            col_high[rows, p * BLK : (p + 1) * BLK] = h
            col_low[rows, p * BLK : (p + 1) * BLK] = l

    def first_cols(n, carry):
        col_unpack(n, lambda rows, there: cols[rows, there])
        return carry

    def dress(j):
        mine = slice(j * TILE, (j + 1) * TILE)

        def one(g, carry):
            if j == 0:
                relay(STEPS + g)
            ch, cl = col_high[mine, :], col_low[mine, :]
            parts_h, parts_l = [], []
            for i in range(2):
                rows = pl.ds(pl.multiple_of(g * PAIR + i * TILE, TILE), TILE)
                bh, bl = high[rows, :], low[rows, :]
                direct = dot_nt(ch, bh) + dot_nt(ch, bl) + dot_nt(cl, bh)
                energy = column_b[mine, :] + (row_a - occ[g * 2 + i])
                h, l = split(-direct / energy)
                parts_h.append(h)
                parts_l.append(l)
            th, tl = jnp.concatenate(parts_h, axis=1), jnp.concatenate(parts_l, axis=1)
            rows = pl.ds(pl.multiple_of(g * PAIR, PAIR), PAIR)
            bh, bl = high[rows, :], low[rows, :]
            total[mine, :] += dot_nn(th, bh) + dot_nn(th, bl) + dot_nn(tl, bh)
            return carry

        lax.fori_loop(2 * j, 2 * j + 2, first_cols, 0)
        total[mine, :] = jnp.zeros((TILE, NAUX), F32)
        lax.fori_loop(0, 4, one, 0)

    def pack(n, carry):
        rows = pl.ds(pl.multiple_of(n * BLK, BLK), BLK)
        for k in range(PRESENT):
            part[rows, k * BLK : (k + 1) * BLK] = slot_of(n, k, lambda p: total[rows, p * BLK : (p + 1) * BLK])
        return carry

    def put(src, dst, s, r, **device):
        return pltpu.make_async_remote_copy(src, dst, s, r, device_id=device, device_id_type=MESH)

    def piece(j, owner):
        return pl.ds(pl.multiple_of(j * TILE + owner * HALF, HALF), HALF)

    def home(member):
        return jnp.where(member == vb, aux, 4)

    here = home(va)
    source = va == vb
    sends = []

    def scatter(j):
        lax.fori_loop(2 * j, 2 * j + 2, pack, 0)
        for k in ORDER:
            target = (va + k) % 8
            copy = put(part.at[piece(j, target)], recv.at[j, k - 1], rs_s.at[j, k - 1], rs_r.at[j, k - 1], va=target)
            copy.start()
            sends.append(copy)

    def gather(j):
        for k in range(7):
            put(recv.at[j, k], recv.at[j, k], rs_s.at[j, k], rs_r.at[j, k], va=va).wait_recv()
        rows = piece(j, va)
        value = ((recv[j, 0] + recv[j, 1]) + (recv[j, 2] + recv[j, 3])) + ((recv[j, 4] + recv[j, 5]) + recv[j, 6])
        buf[here, rows] = part[rows] + value

        @pl.when(jnp.logical_not(source))
        def _():
            deliver(j, va, vb, 0).start()

    def deliver(j, owner, target, n):
        rows = piece(j, owner)
        return put(buf.at[here, rows], buf.at[home(target), rows], ag_s.at[j, n], ag_r.at[j, owner], va=target)

    side = x * 2 + 1 - y
    row_mates = [m * 2 + y for m in (across, right, left)]

    def deliveries(act):
        for j in range(2):
            for n, target in enumerate((side, *row_mates)):

                @pl.when(target != vb)
                def _():
                    act(j, va, target, 1 + n)

    def passed_on(j, act):
        for n, target in enumerate(row_mates):

            @pl.when(target != vb)
            def _():
                act(j, side, target, 5 + n)

    def gathered(j, owner):
        ref = buf.at[here, piece(j, owner)]
        put(ref, ref, ag_s.at[j, 0], ag_r.at[j, owner], va=va).wait_recv()

    dress(0)
    scatter(0)
    dress(1)
    scatter(1)
    gather(0)

    up, down = (vb + 1) % 8, (vb + 7) % 8
    distances = ((vb - va + 8) % 8, (va - vb + 8) % 8)
    owners = (va, x * 2 + 1 - y, *(m * 2 + yy for yy in (y, 1 - y) for m in (right, left)), across * 2 + y, across * 2 + 1 - y)

    def owner_of(step, way):
        owner = owners[6 + way]
        for n in range(3):
            owner = jnp.where(step % 4 == n, owners[2 * n + way], owner)
        return owner

    def chunk_rows(step, way):
        return piece(step // 4, owner_of(step, way))

    def ring(group, step, way, sems, **device):
        ref = buf.at[group, chunk_rows(step, way)]
        return put(ref, ref, sems[0].at[way, step], sems[1].at[way, step], **device)

    pair_sems, far_sems, last_sems = (pair_s, pair_r), (far_s, far_r), (last_s, last_r)
    lags = [(RING_LAG * d) // 2 for d in distances]
    def ring_step(t, carry):
        for way in range(2):
            step = t - lags[way]
            toward = (up, down)[way]

            @pl.when((step >= 0) & (step < RING + EARLY))
            def _():
                late = step >= RING
                local = jnp.where(late, step - RING, step)
                ref = buf.at[jnp.where(late, far, aux), chunk_rows(local, way)]
                along = put(ref, ref, ring_s.at[way, step], ring_r.at[way, step], vb=toward)

                @pl.when(jnp.logical_not(source))
                def _():
                    along.wait_recv()

                @pl.when(source & late)
                def _():
                    ring(far, local, way, far_sems, va=va).wait_recv()

                @pl.when(source & jnp.logical_not(late) & ((step % 4 != 0) | ((way == 1) & (step == 0))))
                def _():
                    gathered(local // 4, owner_of(local, way))

                @pl.when(distances[way] < 7)
                def _():
                    along.start()

                @pl.when(jnp.logical_not(late))
                def _():
                    @pl.when(source | (step >= EARLY))
                    def _():
                        ring(aux, local, way, far_sems, aux=far).start()

                    ring(aux, local, way, pair_sems, aux=partner).start()

                @pl.when(late)
                def _():
                    ring(far, local, way, last_sems, aux=partner).start()

        return carry

    @pl.when(source)
    def _():
        ring_step(0, 0)

    gather(1)
    deliveries(lambda *which: deliver(*which).start())

    @pl.when(source)
    def _():
        lax.fori_loop(1, 4, ring_step, 0)

    @pl.when(jnp.logical_not(source))
    def _():
        gathered(0, side)

    passed_on(0, lambda *which: deliver(*which).start())
    gathered(1, side)
    passed_on(1, lambda *which: deliver(*which).start())

    def later_step(t, carry):
        @pl.when(jnp.logical_not(source) | (t >= 4))
        def _():
            ring_step(t, 0)

        return carry

    lax.fori_loop(1, RING + EARLY + (RING_LAG * 7) // 2, later_step, 0)

    @pl.when(jnp.logical_not(source))
    def _():
        for j in range(2):
            for owner in owners[2:]:
                gathered(j, owner)

    def second_cols(n, carry):
        col_unpack(n, lambda rows, there: cols[rows, there] + 2.0 * buf[here, rows, there])
        return carry

    lax.fori_loop(0, 4, second_cols, 0)

    def residual(group):
        for i in range(2):
            orbital = group * 2 + i
            for half in range(2):
                rows = pl.ds(pl.multiple_of(orbital * TILE + half * BLK, BLK), BLK)
                here_rows = pl.ds(i * TILE + half * BLK, BLK)
                for p in range(NPB):
                    block = slice(p * BLK, (p + 1) * BLK)
                    value = high[rows, block].astype(F32) + low[rows, block].astype(F32)
                    change = block_of(
                        row_weights, orbital * 2 + half, p, lambda s: buf[group, here_rows, s * BLK : (s + 1) * BLK]
                    )
                    h, l = split(value + 2.0 * change)
                    row_high[half * BLK : (half + 1) * BLK, block] = h
                    row_low[half * BLK : (half + 1) * BLK, block] = l
            rh, rl = row_high[...], row_low[...]
            ch, cl = col_high[...], col_low[...]
            result = dot_nt(rh, ch) + dot_nt(rh, cl) + dot_nt(rl, ch)
            result = -result / ((column_a - occ[orbital]) + row_b)
            for n in range(4):
                place = pl.ds(orbital * (4 * TILE) + n % 2 * 2 + n // 2, TILE, stride=4)
                out[place, :] = result[:, n * BLK : (n + 1) * BLK]

    def wait_chunks(group, sems):
        def one(step, carry):
            for way in range(2):
                ring(group, step, way, sems, va=va).wait_recv()
            return carry

        lax.fori_loop(0, RING, one, 0)

    def phase(n, carry):
        group = jnp.where(n == 0, aux, jnp.where(n == 1, partner, jnp.where(n == 2, far, corner)))

        @pl.when(n == 1)
        def _():
            def onward(step, carry):
                for way in range(2):
                    ring(far, step, way, far_sems, va=va).wait_recv()
                    ring(far, step, way, last_sems, aux=partner).start()
                return carry

            lax.fori_loop(EARLY, RING, onward, 0)
            wait_chunks(partner, pair_sems)

        @pl.when(n == 3)
        def _():
            wait_chunks(corner, last_sems)

        residual(group)
        return carry

    lax.fori_loop(0, 4, phase, 0)

    def ring_drain(step, carry):
        for way in range(2):

            @pl.when(step < RING)
            def _():
                ring(aux, step, way, pair_sems, aux=partner).wait_send()
                ring(far, step, way, last_sems, aux=partner).wait_send()

                @pl.when(source | (step >= EARLY))
                def _():
                    ring(aux, step, way, far_sems, aux=far).wait_send()

            @pl.when(distances[way] < 7)
            def _():
                ref = buf.at[aux, chunk_rows(0, way)]
                put(ref, ref, ring_s.at[way, step], ring_r.at[way, step], vb=up).wait_send()

        return carry

    lax.fori_loop(0, RING + EARLY, ring_drain, 0)
    lax.fori_loop(0, CHUNKS, spread_drain, 0)
    for copy in sends:
        copy.wait_send()
    for j in range(2):

        @pl.when(jnp.logical_not(source))
        def _():
            deliver(j, va, vb, 0).wait_send()

        passed_on(j, lambda *which: deliver(*which).wait_send())
    deliveries(lambda *which: deliver(*which).wait_send())


def body(factors, domains, occ_energy, vir_energy):
    smem = pl.BlockSpec(memory_space=pltpu.SMEM)
    vmem = pl.BlockSpec(memory_space=pltpu.VMEM)
    dma = pltpu.SemaphoreType.DMA
    out = pl.pallas_call(
        kernel,
        out_shape=jax.ShapeDtypeStruct((ROWS * 4, BLK), F32),
        in_specs=[smem, smem, vmem, pl.BlockSpec(memory_space=pltpu.HBM)],
        out_specs=vmem,
        scratch_shapes=[
            pltpu.VMEM((2, NAUX * O, BLK), F32),
            pltpu.VMEM((ROWS, NAUX), BF16),
            pltpu.VMEM((ROWS, NAUX), BF16),
            pltpu.VMEM((PAIR, PACK), F32),
            pltpu.VMEM((PAIR, NAUX), BF16),
            pltpu.VMEM((PAIR, NAUX), BF16),
            pltpu.VMEM((PAIR, NAUX), F32),
            pltpu.VMEM((PAIR, PACK), F32),
            pltpu.VMEM((5, PAIR, PACK), F32),
            pltpu.VMEM((2, 7, HALF, PACK), F32),
            pltpu.VMEM((TILE, NAUX), BF16),
            pltpu.VMEM((TILE, NAUX), BF16),
            pltpu.SMEM((O * 2 * NPB * 3,), F32),
            pltpu.SMEM((4 * NPB * 3,), F32),
            dma((NPB, 2)), dma((3, CHUNKS, 2)), dma((3, CHUNKS)),
            dma((2, 7)), dma((2, 7)), dma((2, 8)), dma((2, 8)),
            dma((2, RING + EARLY)), dma((2, RING + EARLY)), dma((2, RING)), dma((2, RING)), dma((2, RING)), dma((2, RING)), dma((2, RING)), dma((2, RING)),
        ],
        compiler_params=pltpu.CompilerParams(collective_id=0, has_side_effects=True, vmem_limit_bytes=VMEM_LIMIT),
        name="amplitudes",
    )(domains.transpose(0, 2, 1), occ_energy, vir_energy.reshape(NVB, BLK), factors.reshape(NAUX * O, TILE))
    return (out * SCALE).reshape(O, TILE, 2, 2, BLK).transpose(0, 1, 3, 2, 4).reshape(O, TILE, 2, TILE)


def solution(mesh):
    placed = (P(None, None, "va"), P(), P(), P())
    return jax.shard_map(
        body, mesh=mesh, in_specs=placed, out_specs=P(None, "va", "aux", "vb"), check_vma=False
    )
```

```python
import math

import jax
import jax.numpy as jnp
from jax import lax
from jax.experimental import pallas as pl
from jax.experimental.pallas import tpu as pltpu
from jax.sharding import PartitionSpec as P

O = 8
V = 2048
NAUX = 1024
BLK = 128
PRESENT = 6
NPB = 8
NVB = 16
TILE = 256
ROWS = O * TILE
PAIR = 2 * TILE
PACK = PRESENT * BLK
SLICE = PAIR // 8
HALF = SLICE // 2
CHUNKS = 8
STEPS = 16
LEAD = 5
RING = 8
EARLY = 1
ORDER = (4, 3, 5, 2, 6, 1, 7)
LAG = 2
RING_LAG = 4
SCALE = 8.0 * O * V / math.sqrt(NAUX)
MESH = pl.DeviceIdType.MESH
F32 = jnp.float32
BF16 = jnp.bfloat16
VMEM_LIMIT = 48 * 1024 * 1024

TREES = (
    {0: (1,), 1: (2, 5), 2: (3, 6), 5: (4,), 6: (7,)},
    {0: (3,), 3: (2, 7), 2: (1,), 7: (4, 6), 6: (5,)},
    {0: (4,), 4: (5, 7), 5: (6, 1), 6: (2,), 7: (3,)},
)


def split(value):
    high = value.astype(BF16)
    return high, (value - high.astype(F32)).astype(BF16)


def dot_nt(left, right):
    return lax.dot_general(left, right, (((1,), (1,)), ((), ())), preferred_element_type=F32)


def dot_nn(left, right):
    return lax.dot_general(left, right, (((1,), (0,)), ((), ())), preferred_element_type=F32)


def kernel(
    domains, occ, vir, factors, out,
    raw, high, low, cols, col_high, col_low, total, part, buf, recv, row_high, row_low,
    row_weights, col_weights,
    load, spread_s, spread_r,
    rs_s, rs_r, ag_s, ag_r, ring_s, ring_r, pair_s, pair_r, far_s, far_r, last_s, last_r,
):
    va, vb, aux = lax.axis_index("va"), lax.axis_index("vb"), lax.axis_index("aux")
    x, y = va // 2, va % 2
    core, hi = aux % 2, aux // 2
    right, left, across = (x + 1) % 4, (x + 3) % 4, (x + 2) % 4
    partner, far, corner = hi * 2 + (1 - core), (aux + 2) % 4, ((1 - hi) * 2) + (1 - core)

    barrier = pltpu.get_barrier_semaphore()
    for k in range(1, 8):
        pl.semaphore_signal(barrier, 1, device_id={"va": (va + k) % 8}, device_id_type=MESH)
    pl.semaphore_signal(barrier, 1, device_id={"vb": (vb + 1) % 8}, device_id_type=MESH)
    pl.semaphore_signal(barrier, 1, device_id={"vb": (vb + 7) % 8}, device_id_type=MESH)
    pl.semaphore_signal(barrier, 1, device_id={"aux": partner}, device_id_type=MESH)
    pl.semaphore_signal(barrier, 1, device_id={"aux": far}, device_id_type=MESH)

    def fetch(p, half):
        rows = pl.ds(p * BLK * O, BLK * O)
        return pltpu.make_async_copy(factors.at[rows, pl.ds(half * BLK, BLK)], raw.at[half, rows], load.at[p, half])

    for p in range(NPB):
        for half in range(2):
            fetch(p, half).start()

    def weigh(table, n, i, block):
        absent = jnp.float32(0)
        for p in range(NPB):
            keep = domains[i, p, block].astype(F32)
            table[(n * NPB + p) * 3] = keep * (1.0 - absent) * (2.0 - absent) * 0.5
            table[(n * NPB + p) * 3 + 1] = keep * absent * (2.0 - absent)
            table[(n * NPB + p) * 3 + 2] = keep * absent * (absent - 1.0) * 0.5
            absent += 1.0 - keep

    def row_tables(n, carry):
        weigh(row_weights, n, n // 2, va * 2 + n % 2)
        return carry

    def col_tables(n, carry):
        weigh(col_weights, n, aux * 2 + n // 2, vb * 2 + n % 2)
        return carry

    lax.fori_loop(0, O * 2, row_tables, 0)
    lax.fori_loop(0, 4, col_tables, 0)

    def slot_of(n, k, full):
        values = [col_weights[(n * NPB + k + d) * 3 + d] * full(k + d) for d in range(3)]
        return values[0] + values[1] + values[2]

    def block_of(table, n, p, slots):
        values = [table[(n * NPB + p) * 3 + d] * slots(p - d) for d in range(3) if 0 <= p - d < PRESENT]
        return sum(values[1:], values[0])

    def lanes(slot):
        return pl.ds(pl.multiple_of(slot * BLK, BLK), BLK)

    def turned(i, half, p):
        keep = domains[i, p, va * 2 + half].astype(F32)
        return raw[half, pl.ds(p * (BLK * O) + i, BLK, stride=O), :].T * keep

    root_x, root_y = vb // 2, vb % 2
    node = (x - root_x + 4) % 4 + 4 * ((y + root_y) % 2)

    for p in range(NPB):
        for half in range(2):
            fetch(p, half).wait()

    @pl.when(node == 0)
    def _():
        def own(n, carry):
            i, half = aux * 2 + n // 2, n % 2
            rows = pl.ds(pl.multiple_of(n * BLK, BLK), BLK)
            for p in range(NPB):
                total[rows, p * BLK : (p + 1) * BLK] = turned(i, half, p)
            for k in range(PRESENT):
                cols[rows, k * BLK : (k + 1) * BLK] = slot_of(n, k, lambda p: total[rows, p * BLK : (p + 1) * BLK])
            return carry

        lax.fori_loop(0, 4, own, 0)

    def lookup(values):
        found = jnp.int32(values[0])
        for n in range(1, 8):
            found = jnp.where(node == n, jnp.int32(values[n]), found)
        return found

    skews, childs = [], []
    for tree in TREES:
        depth = {0: 0}
        todo = [0]
        for n in todo:
            for member in tree.get(n, ()):
                depth[member] = depth[n] + 1
                todo.append(member)
        skews.append(lookup([LEAD + LAG * (depth[n] - 1) for n in range(8)]))
        childs.append([lookup([(*tree.get(n, ()), -1, -1)[k] for n in range(8)]) for k in range(2)])

    def spread(tree, chunk, child, member):
        ref = cols.at[pl.ds(pl.multiple_of(chunk * SLICE, SLICE), SLICE), pl.ds(tree * 256, 256)]
        place = ((root_x + member % 4) % 4) * 2 + (root_y + member // 4) % 2
        return pltpu.make_async_remote_copy(
            ref, ref, spread_s.at[tree, chunk, child], spread_r.at[tree, chunk], device_id={"va": place}, device_id_type=MESH
        )

    pl.semaphore_wait(barrier, 11)

    @pl.when(node == 0)
    def _():
        def launch(chunk, carry):
            for tree in range(3):
                spread(tree, chunk, 0, childs[tree][0]).start()
            return carry

        lax.fori_loop(0, CHUNKS, launch, 0)

    def relay(t):
        for tree in range(3):
            chunk = t - skews[tree]

            @pl.when((node != 0) & (chunk >= 0) & (chunk < CHUNKS))
            def _():
                spread(tree, chunk, 0, 0).wait_recv()
                for k in range(2):
                    member = childs[tree][k]

                    @pl.when(member >= 0)
                    def _():
                        spread(tree, chunk, k, member).start()

    def prepare(t, carry):
        relay(t)
        p = t // 2
        for n in range(4):
            i = (t % 2) * 4 + n
            for half in range(2):
                h, l = split(turned(i, half, p))
                rows = pl.ds(pl.multiple_of(i * TILE + half * BLK, BLK), BLK)
                high[rows, lanes(p)] = h
                low[rows, lanes(p)] = l
        return carry

    lax.fori_loop(0, STEPS, prepare, 0)

    def spread_drain(chunk, carry):
        for tree in range(3):
            for k in range(2):
                member = childs[tree][k]

                @pl.when(member >= 0)
                def _():
                    spread(tree, chunk, k, member).wait_send()

        return carry

    def energy_row(tile):
        return [vir[pl.ds(tile * 2 + half, 1), :] for half in range(2)]

    def energy_column(rows):
        return jnp.concatenate([jnp.broadcast_to(row, (8, BLK)).T[:, :1] for row in rows], axis=0)

    rows_a, rows_b = energy_row(va), energy_row(vb)
    row_a = jnp.concatenate(rows_a, axis=1)
    occ_j = [occ[aux * 2 + j] for j in range(2)]
    row_b = jnp.concatenate([row - occ_j[j] for j in range(2) for row in rows_b], axis=1)
    column_a = energy_column(rows_a)
    column_b = energy_column([row - occ_j[j] for j in range(2) for row in rows_b])

    def col_unpack(n, extra):
        rows = pl.ds(pl.multiple_of(n * BLK, BLK), BLK)
        for p in range(NPB):
            h, l = split(block_of(col_weights, n, p, lambda s: extra(rows, slice(s * BLK, (s + 1) * BLK))))
            col_high[rows, p * BLK : (p + 1) * BLK] = h
            col_low[rows, p * BLK : (p + 1) * BLK] = l

    def first_cols(n, carry):
        col_unpack(n, lambda rows, there: cols[rows, there])
        return carry

    def dress(j):
        mine = slice(j * TILE, (j + 1) * TILE)

        def one(g, carry):
            if j == 0:
                relay(STEPS + g)
            ch, cl = col_high[mine, :], col_low[mine, :]
            parts_h, parts_l = [], []
            for i in range(2):
                rows = pl.ds(pl.multiple_of(g * PAIR + i * TILE, TILE), TILE)
                bh, bl = high[rows, :], low[rows, :]
                direct = dot_nt(ch, bh) + dot_nt(ch, bl) + dot_nt(cl, bh)
                energy = column_b[mine, :] + (row_a - occ[g * 2 + i])
                h, l = split(-direct / energy)
                parts_h.append(h)
                parts_l.append(l)
            th, tl = jnp.concatenate(parts_h, axis=1), jnp.concatenate(parts_l, axis=1)
            rows = pl.ds(pl.multiple_of(g * PAIR, PAIR), PAIR)
            bh, bl = high[rows, :], low[rows, :]
            total[mine, :] += dot_nn(th, bh) + dot_nn(th, bl) + dot_nn(tl, bh)
            return carry

        lax.fori_loop(2 * j, 2 * j + 2, first_cols, 0)
        total[mine, :] = jnp.zeros((TILE, NAUX), F32)
        lax.fori_loop(0, 4, one, 0)

    def pack(n, carry):
        rows = pl.ds(pl.multiple_of(n * BLK, BLK), BLK)
        for k in range(PRESENT):
            part[rows, k * BLK : (k + 1) * BLK] = slot_of(n, k, lambda p: total[rows, p * BLK : (p + 1) * BLK])
        return carry

    def put(src, dst, s, r, **device):
        return pltpu.make_async_remote_copy(src, dst, s, r, device_id=device, device_id_type=MESH)

    def piece(j, owner):
        return pl.ds(pl.multiple_of(j * TILE + owner * HALF, HALF), HALF)

    def home(member):
        return jnp.where(member == vb, aux, 4)

    here = home(va)
    sends = []

    def scatter(j):
        lax.fori_loop(2 * j, 2 * j + 2, pack, 0)
        for k in ORDER:
            target = (va + k) % 8
            copy = put(part.at[piece(j, target)], recv.at[j, k - 1], rs_s.at[j, k - 1], rs_r.at[j, k - 1], va=target)
            copy.start()
            sends.append(copy)

    def gather(j):
        for k in range(7):
            put(recv.at[j, k], recv.at[j, k], rs_s.at[j, k], rs_r.at[j, k], va=va).wait_recv()
        rows = piece(j, va)
        value = ((recv[j, 0] + recv[j, 1]) + (recv[j, 2] + recv[j, 3])) + ((recv[j, 4] + recv[j, 5]) + recv[j, 6])
        buf[here, rows] = part[rows] + value
        for k in ORDER:
            target = (va + k) % 8
            copy = put(buf.at[here, rows], buf.at[home(target), rows], ag_s.at[j, k - 1], ag_r.at[j, va], va=target)
            copy.start()
            sends.append(copy)

    def gathered(j, owner):
        ref = buf.at[here, piece(j, owner)]
        put(ref, ref, ag_s.at[j, 0], ag_r.at[j, owner], va=va).wait_recv()

    dress(0)
    scatter(0)
    dress(1)
    scatter(1)
    gather(0)

    up, down = (vb + 1) % 8, (vb + 7) % 8
    distances = ((vb - va + 8) % 8, (va - vb + 8) % 8)
    owners = (va, x * 2 + 1 - y, *(m * 2 + yy for yy in (y, 1 - y) for m in (right, left)), across * 2 + y, across * 2 + 1 - y)

    def owner_of(step, way):
        owner = owners[6 + way]
        for n in range(3):
            owner = jnp.where(step % 4 == n, owners[2 * n + way], owner)
        return owner

    def chunk_rows(step, way):
        return piece(step // 4, owner_of(step, way))

    def ring(group, step, way, sems, **device):
        ref = buf.at[group, chunk_rows(step, way)]
        return put(ref, ref, sems[0].at[way, step], sems[1].at[way, step], **device)

    pair_sems, far_sems, last_sems = (pair_s, pair_r), (far_s, far_r), (last_s, last_r)
    lags = [(RING_LAG * d) // 2 for d in distances]
    source = va == vb

    def ring_step(t, carry):
        for way in range(2):
            step = t - lags[way]
            toward = (up, down)[way]

            @pl.when((step >= 0) & (step < RING + EARLY))
            def _():
                late = step >= RING
                local = jnp.where(late, step - RING, step)
                ref = buf.at[jnp.where(late, far, aux), chunk_rows(local, way)]
                along = put(ref, ref, ring_s.at[way, step], ring_r.at[way, step], vb=toward)

                @pl.when(jnp.logical_not(source))
                def _():
                    along.wait_recv()

                @pl.when(source & late)
                def _():
                    ring(far, local, way, far_sems, va=va).wait_recv()

                @pl.when(source & jnp.logical_not(late) & ((step % 4 != 0) | (way != 0)))
                def _():
                    gathered(local // 4, owner_of(local, way))

                @pl.when(distances[way] < 7)
                def _():
                    along.start()

                @pl.when(jnp.logical_not(late))
                def _():
                    @pl.when(source | (step >= EARLY))
                    def _():
                        ring(aux, local, way, far_sems, aux=far).start()

                    ring(aux, local, way, pair_sems, aux=partner).start()

                @pl.when(late)
                def _():
                    ring(far, local, way, last_sems, aux=partner).start()

        return carry

    @pl.when(source)
    def _():
        ring_step(0, 0)

    gather(1)
    lax.fori_loop(1, RING + EARLY + (RING_LAG * 7) // 2, ring_step, 0)

    @pl.when(jnp.logical_not(source))
    def _():
        for j in range(2):
            for owner in owners[1:]:
                gathered(j, owner)

    def second_cols(n, carry):
        col_unpack(n, lambda rows, there: cols[rows, there] + 2.0 * buf[here, rows, there])
        return carry

    lax.fori_loop(0, 4, second_cols, 0)

    def residual(group):
        for i in range(2):
            orbital = group * 2 + i
            for half in range(2):
                rows = pl.ds(pl.multiple_of(orbital * TILE + half * BLK, BLK), BLK)
                here_rows = pl.ds(i * TILE + half * BLK, BLK)
                for p in range(NPB):
                    block = slice(p * BLK, (p + 1) * BLK)
                    value = high[rows, block].astype(F32) + low[rows, block].astype(F32)
                    change = block_of(
                        row_weights, orbital * 2 + half, p, lambda s: buf[group, here_rows, s * BLK : (s + 1) * BLK]
                    )
                    h, l = split(value + 2.0 * change)
                    row_high[i, half * BLK : (half + 1) * BLK, block] = h
                    row_low[i, half * BLK : (half + 1) * BLK, block] = l
        for i in range(2):
            orbital = group * 2 + i
            rh, rl = row_high[i], row_low[i]
            ch, cl = col_high[...], col_low[...]
            result = dot_nt(rh, ch) + dot_nt(rh, cl) + dot_nt(rl, ch)
            result = -result / ((column_a - occ[orbital]) + row_b)
            for n in range(4):
                place = pl.ds(orbital * (4 * TILE) + n % 2 * 2 + n // 2, TILE, stride=4)
                out[place, :] = result[:, n * BLK : (n + 1) * BLK]

    def wait_chunks(group, sems):
        def one(step, carry):
            for way in range(2):
                ring(group, step, way, sems, va=va).wait_recv()
            return carry

        lax.fori_loop(0, RING, one, 0)

    def phase(n, carry):
        group = jnp.where(n == 0, aux, jnp.where(n == 1, partner, jnp.where(n == 2, far, corner)))

        @pl.when(n == 1)
        def _():
            def onward(step, carry):
                for way in range(2):
                    ring(far, step, way, far_sems, va=va).wait_recv()
                    ring(far, step, way, last_sems, aux=partner).start()
                return carry

            lax.fori_loop(EARLY, RING, onward, 0)
            wait_chunks(partner, pair_sems)

        @pl.when(n == 3)
        def _():
            wait_chunks(corner, last_sems)

        residual(group)
        return carry

    lax.fori_loop(0, 4, phase, 0)

    def ring_drain(step, carry):
        for way in range(2):

            @pl.when(step < RING)
            def _():
                ring(aux, step, way, pair_sems, aux=partner).wait_send()
                ring(far, step, way, last_sems, aux=partner).wait_send()

                @pl.when(source | (step >= EARLY))
                def _():
                    ring(aux, step, way, far_sems, aux=far).wait_send()

            @pl.when(distances[way] < 7)
            def _():
                ref = buf.at[aux, chunk_rows(0, way)]
                put(ref, ref, ring_s.at[way, step], ring_r.at[way, step], vb=up).wait_send()

        return carry

    lax.fori_loop(0, RING + EARLY, ring_drain, 0)
    lax.fori_loop(0, CHUNKS, spread_drain, 0)
    for copy in sends:
        copy.wait_send()


def body(factors, domains, occ_energy, vir_energy):
    smem = pl.BlockSpec(memory_space=pltpu.SMEM)
    vmem = pl.BlockSpec(memory_space=pltpu.VMEM)
    dma = pltpu.SemaphoreType.DMA
    inputs = (domains.transpose(0, 2, 1), occ_energy, vir_energy.reshape(NVB, BLK), factors.reshape(NAUX * O, TILE))
    inputs = [pltpu.with_memory_space_constraint(array, pltpu.HBM) for array in inputs]
    out = pl.pallas_call(
        kernel,
        out_shape=jax.ShapeDtypeStruct((ROWS * 4, BLK), F32),
        in_specs=[smem, smem, vmem, pl.BlockSpec(memory_space=pltpu.HBM)],
        out_specs=vmem,
        scratch_shapes=[
            pltpu.VMEM((2, NAUX * O, BLK), F32),
            pltpu.VMEM((ROWS, NAUX), BF16),
            pltpu.VMEM((ROWS, NAUX), BF16),
            pltpu.VMEM((PAIR, PACK), F32),
            pltpu.VMEM((PAIR, NAUX), BF16),
            pltpu.VMEM((PAIR, NAUX), BF16),
            pltpu.VMEM((PAIR, NAUX), F32),
            pltpu.VMEM((PAIR, PACK), F32),
            pltpu.VMEM((5, PAIR, PACK), F32),
            pltpu.VMEM((2, 7, HALF, PACK), F32),
            pltpu.VMEM((2, TILE, NAUX), BF16),
            pltpu.VMEM((2, TILE, NAUX), BF16),
            pltpu.SMEM((O * 2 * NPB * 3,), F32),
            pltpu.SMEM((4 * NPB * 3,), F32),
            dma((NPB, 2)), dma((3, CHUNKS, 2)), dma((3, CHUNKS)),
            dma((2, 7)), dma((2, 7)), dma((2, 7)), dma((2, 8)),
            dma((2, RING + EARLY)), dma((2, RING + EARLY)), dma((2, RING)), dma((2, RING)), dma((2, RING)), dma((2, RING)), dma((2, RING)), dma((2, RING)),
        ],
        compiler_params=pltpu.CompilerParams(collective_id=0, has_side_effects=True, vmem_limit_bytes=VMEM_LIMIT),
        name="amplitudes",
    )(*inputs)
    return (out * SCALE).reshape(O, TILE, 2, 2, BLK).transpose(0, 1, 3, 2, 4).reshape(O, TILE, 2, TILE)


def solution(mesh):
    placed = (P(None, None, "va"), P(), P(), P())
    return jax.shard_map(
        body, mesh=mesh, in_specs=placed, out_specs=P(None, "va", "aux", "vb"), check_vma=False
    )
```

```python
import math

import jax
import jax.numpy as jnp
from jax import lax
from jax.experimental import pallas as pl
from jax.experimental.pallas import tpu as pltpu
from jax.sharding import PartitionSpec as P

O = 8
V = 2048
NAUX = 1024
BLK = 128
PRESENT = 6
NPB = 8
NVB = 16
TILE = 256
ROWS = O * TILE
PAIR = 2 * TILE
PACK = PRESENT * BLK
SLICE = PAIR // 8
HALF = SLICE // 2
CHUNKS = 8
STEPS = 16
LEAD = 5
RING = 8
EARLY = 0
ORDER = (4, 3, 5, 2, 6, 1, 7)
LAG = 2
RING_LAG = 4
SCALE = 8.0 * O * V / math.sqrt(NAUX)
MESH = pl.DeviceIdType.MESH
F32 = jnp.float32
BF16 = jnp.bfloat16
VMEM_LIMIT = 48 * 1024 * 1024

TREES = (
    {0: (1,), 1: (2, 5), 2: (3, 6), 5: (4,), 6: (7,)},
    {0: (3,), 3: (2, 7), 2: (1,), 7: (4, 6), 6: (5,)},
    {0: (4,), 4: (5, 7), 5: (6, 1), 6: (2,), 7: (3,)},
)


def split(value):
    high = value.astype(BF16)
    return high, (value - high.astype(F32)).astype(BF16)


def dot_nt(left, right):
    return lax.dot_general(left, right, (((1,), (1,)), ((), ())), preferred_element_type=F32)


def dot_nn(left, right):
    return lax.dot_general(left, right, (((1,), (0,)), ((), ())), preferred_element_type=F32)


def kernel(
    domains, occ, vir, factors, out,
    raw, high, low, cols, col_high, col_low, total, part, buf, recv, row_high, row_low,
    row_weights, col_weights,
    load, spread_s, spread_r,
    rs_s, rs_r, ag_s, ag_r, ring_s, ring_r, pair_s, pair_r, far_s, far_r, last_s, last_r,
):
    va, vb, aux = lax.axis_index("va"), lax.axis_index("vb"), lax.axis_index("aux")
    x, y = va // 2, va % 2
    core, hi = aux % 2, aux // 2
    right, left, across = (x + 1) % 4, (x + 3) % 4, (x + 2) % 4
    partner, far, corner = hi * 2 + (1 - core), (aux + 2) % 4, ((1 - hi) * 2) + (1 - core)

    barrier = pltpu.get_barrier_semaphore()
    for k in range(1, 8):
        pl.semaphore_signal(barrier, 1, device_id={"va": (va + k) % 8}, device_id_type=MESH)
    pl.semaphore_signal(barrier, 1, device_id={"vb": (vb + 1) % 8}, device_id_type=MESH)
    pl.semaphore_signal(barrier, 1, device_id={"vb": (vb + 7) % 8}, device_id_type=MESH)
    pl.semaphore_signal(barrier, 1, device_id={"aux": partner}, device_id_type=MESH)
    pl.semaphore_signal(barrier, 1, device_id={"aux": far}, device_id_type=MESH)

    def fetch(p, half):
        rows = pl.ds(p * BLK * O, BLK * O)
        return pltpu.make_async_copy(factors.at[rows, pl.ds(half * BLK, BLK)], raw.at[half, rows], load.at[p, half])

    for p in range(NPB):
        for half in range(2):
            fetch(p, half).start()

    def weigh(table, n, i, block):
        absent = jnp.float32(0)
        for p in range(NPB):
            keep = domains[i, p, block].astype(F32)
            table[(n * NPB + p) * 3] = keep * (1.0 - absent) * (2.0 - absent) * 0.5
            table[(n * NPB + p) * 3 + 1] = keep * absent * (2.0 - absent)
            table[(n * NPB + p) * 3 + 2] = keep * absent * (absent - 1.0) * 0.5
            absent += 1.0 - keep

    def row_tables(n, carry):
        weigh(row_weights, n, n // 2, va * 2 + n % 2)
        return carry

    def col_tables(n, carry):
        weigh(col_weights, n, aux * 2 + n // 2, vb * 2 + n % 2)
        return carry

    lax.fori_loop(0, O * 2, row_tables, 0)
    lax.fori_loop(0, 4, col_tables, 0)

    def slot_of(n, k, full):
        values = [col_weights[(n * NPB + k + d) * 3 + d] * full(k + d) for d in range(3)]
        return values[0] + values[1] + values[2]

    def block_of(table, n, p, slots):
        values = [table[(n * NPB + p) * 3 + d] * slots(p - d) for d in range(3) if 0 <= p - d < PRESENT]
        return sum(values[1:], values[0])

    def lanes(slot):
        return pl.ds(pl.multiple_of(slot * BLK, BLK), BLK)

    def turned(i, half, p):
        keep = domains[i, p, va * 2 + half].astype(F32)
        return raw[half, pl.ds(p * (BLK * O) + i, BLK, stride=O), :].T * keep

    root_x, root_y = vb // 2, vb % 2
    node = (x - root_x + 4) % 4 + 4 * ((y + root_y) % 2)

    for p in range(NPB):
        for half in range(2):
            fetch(p, half).wait()

    @pl.when(node == 0)
    def _():
        def own(n, carry):
            i, half = aux * 2 + n // 2, n % 2
            rows = pl.ds(pl.multiple_of(n * BLK, BLK), BLK)
            for p in range(NPB):
                total[rows, p * BLK : (p + 1) * BLK] = turned(i, half, p)
            for k in range(PRESENT):
                cols[rows, k * BLK : (k + 1) * BLK] = slot_of(n, k, lambda p: total[rows, p * BLK : (p + 1) * BLK])
            return carry

        lax.fori_loop(0, 4, own, 0)

    def lookup(values):
        found = jnp.int32(values[0])
        for n in range(1, 8):
            found = jnp.where(node == n, jnp.int32(values[n]), found)
        return found

    skews, childs = [], []
    for tree in TREES:
        depth = {0: 0}
        todo = [0]
        for n in todo:
            for member in tree.get(n, ()):
                depth[member] = depth[n] + 1
                todo.append(member)
        skews.append(lookup([LEAD + LAG * (depth[n] - 1) for n in range(8)]))
        childs.append([lookup([(*tree.get(n, ()), -1, -1)[k] for n in range(8)]) for k in range(2)])

    def spread(tree, chunk, child, member):
        ref = cols.at[pl.ds(pl.multiple_of(chunk * SLICE, SLICE), SLICE), pl.ds(tree * 256, 256)]
        place = ((root_x + member % 4) % 4) * 2 + (root_y + member // 4) % 2
        return pltpu.make_async_remote_copy(
            ref, ref, spread_s.at[tree, chunk, child], spread_r.at[tree, chunk], device_id={"va": place}, device_id_type=MESH
        )

    pl.semaphore_wait(barrier, 11)

    @pl.when(node == 0)
    def _():
        def launch(chunk, carry):
            for tree in range(3):
                spread(tree, chunk, 0, childs[tree][0]).start()
            return carry

        lax.fori_loop(0, CHUNKS, launch, 0)

    def relay(t):
        for tree in range(3):
            chunk = t - skews[tree]

            @pl.when((node != 0) & (chunk >= 0) & (chunk < CHUNKS))
            def _():
                spread(tree, chunk, 0, 0).wait_recv()
                for k in range(2):
                    member = childs[tree][k]

                    @pl.when(member >= 0)
                    def _():
                        spread(tree, chunk, k, member).start()

    def prepare(t, carry):
        relay(t)
        p = t // 2
        for n in range(4):
            i = (t % 2) * 4 + n
            for half in range(2):
                h, l = split(turned(i, half, p))
                rows = pl.ds(pl.multiple_of(i * TILE + half * BLK, BLK), BLK)
                high[rows, lanes(p)] = h
                low[rows, lanes(p)] = l
        return carry

    lax.fori_loop(0, STEPS, prepare, 0)

    def spread_drain(chunk, carry):
        for tree in range(3):
            for k in range(2):
                member = childs[tree][k]

                @pl.when(member >= 0)
                def _():
                    spread(tree, chunk, k, member).wait_send()

        return carry

    def energy_row(tile):
        return [vir[pl.ds(tile * 2 + half, 1), :] for half in range(2)]

    def energy_column(rows):
        return jnp.concatenate([jnp.broadcast_to(row, (8, BLK)).T[:, :1] for row in rows], axis=0)

    rows_a, rows_b = energy_row(va), energy_row(vb)
    row_a = jnp.concatenate(rows_a, axis=1)
    occ_j = [occ[aux * 2 + j] for j in range(2)]
    row_b = jnp.concatenate([row - occ_j[j] for j in range(2) for row in rows_b], axis=1)
    column_a = energy_column(rows_a)
    column_b = energy_column([row - occ_j[j] for j in range(2) for row in rows_b])

    def col_unpack(n, extra):
        rows = pl.ds(pl.multiple_of(n * BLK, BLK), BLK)
        for p in range(NPB):
            h, l = split(block_of(col_weights, n, p, lambda s: extra(rows, slice(s * BLK, (s + 1) * BLK))))
            col_high[rows, p * BLK : (p + 1) * BLK] = h
            col_low[rows, p * BLK : (p + 1) * BLK] = l

    def first_cols(n, carry):
        col_unpack(n, lambda rows, there: cols[rows, there])
        return carry

    def dress(j):
        mine = slice(j * TILE, (j + 1) * TILE)

        def one(g, carry):
            if j == 0:
                relay(STEPS + g)
            ch, cl = col_high[mine, :], col_low[mine, :]
            parts_h, parts_l = [], []
            for i in range(2):
                rows = pl.ds(pl.multiple_of(g * PAIR + i * TILE, TILE), TILE)
                bh, bl = high[rows, :], low[rows, :]
                direct = dot_nt(ch, bh) + dot_nt(ch, bl) + dot_nt(cl, bh)
                energy = column_b[mine, :] + (row_a - occ[g * 2 + i])
                h, l = split(-direct / energy)
                parts_h.append(h)
                parts_l.append(l)
            th, tl = jnp.concatenate(parts_h, axis=1), jnp.concatenate(parts_l, axis=1)
            rows = pl.ds(pl.multiple_of(g * PAIR, PAIR), PAIR)
            bh, bl = high[rows, :], low[rows, :]
            total[mine, :] += dot_nn(th, bh) + dot_nn(th, bl) + dot_nn(tl, bh)
            return carry

        lax.fori_loop(2 * j, 2 * j + 2, first_cols, 0)
        total[mine, :] = jnp.zeros((TILE, NAUX), F32)
        lax.fori_loop(0, 4, one, 0)

    def pack(n, carry):
        rows = pl.ds(pl.multiple_of(n * BLK, BLK), BLK)
        for k in range(PRESENT):
            part[rows, k * BLK : (k + 1) * BLK] = slot_of(n, k, lambda p: total[rows, p * BLK : (p + 1) * BLK])
        return carry

    def put(src, dst, s, r, **device):
        return pltpu.make_async_remote_copy(src, dst, s, r, device_id=device, device_id_type=MESH)

    def piece(j, owner):
        return pl.ds(pl.multiple_of(j * TILE + owner * HALF, HALF), HALF)

    def home(member):
        return jnp.where(member == vb, aux, 4)

    here = home(va)
    sends = []

    def scatter(j):
        lax.fori_loop(2 * j, 2 * j + 2, pack, 0)
        for k in ORDER:
            target = (va + k) % 8
            copy = put(part.at[piece(j, target)], recv.at[j, k - 1], rs_s.at[j, k - 1], rs_r.at[j, k - 1], va=target)
            copy.start()
            sends.append(copy)

    def gather(j):
        for k in range(7):
            put(recv.at[j, k], recv.at[j, k], rs_s.at[j, k], rs_r.at[j, k], va=va).wait_recv()
        rows = piece(j, va)
        value = ((recv[j, 0] + recv[j, 1]) + (recv[j, 2] + recv[j, 3])) + ((recv[j, 4] + recv[j, 5]) + recv[j, 6])
        buf[here, rows] = part[rows] + value
        for k in ORDER:
            target = (va + k) % 8
            copy = put(buf.at[here, rows], buf.at[home(target), rows], ag_s.at[j, k - 1], ag_r.at[j, va], va=target)
            copy.start()
            sends.append(copy)

    def gathered(j, owner):
        ref = buf.at[here, piece(j, owner)]
        put(ref, ref, ag_s.at[j, 0], ag_r.at[j, owner], va=va).wait_recv()

    dress(0)
    scatter(0)
    dress(1)
    scatter(1)
    gather(0)

    up, down = (vb + 1) % 8, (vb + 7) % 8
    distances = ((vb - va + 8) % 8, (va - vb + 8) % 8)
    owners = (va, x * 2 + 1 - y, *(m * 2 + yy for yy in (y, 1 - y) for m in (right, left)), across * 2 + y, across * 2 + 1 - y)

    def owner_of(step, way):
        owner = owners[6 + way]
        for n in range(3):
            owner = jnp.where(step % 4 == n, owners[2 * n + way], owner)
        return owner

    def chunk_rows(step, way):
        return piece(step // 4, owner_of(step, way))

    def ring(group, step, way, sems, **device):
        ref = buf.at[group, chunk_rows(step, way)]
        return put(ref, ref, sems[0].at[way, step], sems[1].at[way, step], **device)

    pair_sems, far_sems, last_sems = (pair_s, pair_r), (far_s, far_r), (last_s, last_r)
    lags = [(RING_LAG * d) // 2 for d in distances]
    source = va == vb

    def ring_step(t, carry):
        for way in range(2):
            step = t - lags[way]
            toward = (up, down)[way]

            @pl.when((step >= 0) & (step < RING + EARLY))
            def _():
                late = step >= RING
                local = jnp.where(late, step - RING, step)
                ref = buf.at[jnp.where(late, far, aux), chunk_rows(local, way)]
                along = put(ref, ref, ring_s.at[way, step], ring_r.at[way, step], vb=toward)

                @pl.when(jnp.logical_not(source))
                def _():
                    along.wait_recv()

                @pl.when(source & late)
                def _():
                    ring(far, local, way, far_sems, va=va).wait_recv()

                @pl.when(source & jnp.logical_not(late) & ((step % 4 != 0) | (way != 0)))
                def _():
                    gathered(local // 4, owner_of(local, way))

                @pl.when(distances[way] < 7)
                def _():
                    along.start()

                @pl.when(jnp.logical_not(late))
                def _():
                    @pl.when(source | (step >= EARLY))
                    def _():
                        ring(aux, local, way, far_sems, aux=far).start()

                    ring(aux, local, way, pair_sems, aux=partner).start()

                @pl.when(late)
                def _():
                    ring(far, local, way, last_sems, aux=partner).start()

        return carry

    @pl.when(source)
    def _():
        ring_step(0, 0)

    gather(1)
    lax.fori_loop(1, RING + EARLY + (RING_LAG * 7) // 2, ring_step, 0)

    @pl.when(jnp.logical_not(source))
    def _():
        for j in range(2):
            for owner in owners[1:]:
                gathered(j, owner)

    def second_cols(n, carry):
        col_unpack(n, lambda rows, there: cols[rows, there] + 2.0 * buf[here, rows, there])
        return carry

    lax.fori_loop(0, 4, second_cols, 0)

    def residual(group):
        for i in range(2):
            orbital = group * 2 + i
            for half in range(2):
                rows = pl.ds(pl.multiple_of(orbital * TILE + half * BLK, BLK), BLK)
                here_rows = pl.ds(i * TILE + half * BLK, BLK)
                for p in range(NPB):
                    block = slice(p * BLK, (p + 1) * BLK)
                    value = high[rows, block].astype(F32) + low[rows, block].astype(F32)
                    change = block_of(
                        row_weights, orbital * 2 + half, p, lambda s: buf[group, here_rows, s * BLK : (s + 1) * BLK]
                    )
                    h, l = split(value + 2.0 * change)
                    row_high[i, half * BLK : (half + 1) * BLK, block] = h
                    row_low[i, half * BLK : (half + 1) * BLK, block] = l
        for i in range(2):
            orbital = group * 2 + i
            rh, rl = row_high[i], row_low[i]
            ch, cl = col_high[...], col_low[...]
            result = dot_nt(rh, ch) + dot_nt(rh, cl) + dot_nt(rl, ch)
            result = -result / ((column_a - occ[orbital]) + row_b)
            for n in range(4):
                place = pl.ds(orbital * (4 * TILE) + n % 2 * 2 + n // 2, TILE, stride=4)
                out[place, :] = result[:, n * BLK : (n + 1) * BLK]

    def wait_chunks(group, sems):
        def one(step, carry):
            for way in range(2):
                ring(group, step, way, sems, va=va).wait_recv()
            return carry

        lax.fori_loop(0, RING, one, 0)

    def phase(n, carry):
        group = jnp.where(n == 0, aux, jnp.where(n == 1, partner, jnp.where(n == 2, far, corner)))

        @pl.when(n == 1)
        def _():
            def onward(step, carry):
                for way in range(2):
                    ring(far, step, way, far_sems, va=va).wait_recv()
                    ring(far, step, way, last_sems, aux=partner).start()
                return carry

            lax.fori_loop(EARLY, RING, onward, 0)
            wait_chunks(partner, pair_sems)

        @pl.when(n == 3)
        def _():
            wait_chunks(corner, last_sems)

        residual(group)
        return carry

    lax.fori_loop(0, 4, phase, 0)

    def ring_drain(step, carry):
        for way in range(2):

            @pl.when(step < RING)
            def _():
                ring(aux, step, way, pair_sems, aux=partner).wait_send()
                ring(far, step, way, last_sems, aux=partner).wait_send()

                @pl.when(source | (step >= EARLY))
                def _():
                    ring(aux, step, way, far_sems, aux=far).wait_send()

            @pl.when(distances[way] < 7)
            def _():
                ref = buf.at[aux, chunk_rows(0, way)]
                put(ref, ref, ring_s.at[way, step], ring_r.at[way, step], vb=up).wait_send()

        return carry

    lax.fori_loop(0, RING + EARLY, ring_drain, 0)
    lax.fori_loop(0, CHUNKS, spread_drain, 0)
    for copy in sends:
        copy.wait_send()


def body(factors, domains, occ_energy, vir_energy):
    smem = pl.BlockSpec(memory_space=pltpu.SMEM)
    vmem = pl.BlockSpec(memory_space=pltpu.VMEM)
    dma = pltpu.SemaphoreType.DMA
    inputs = (domains.transpose(0, 2, 1), occ_energy, vir_energy.reshape(NVB, BLK), factors.reshape(NAUX * O, TILE))
    inputs = [pltpu.with_memory_space_constraint(array, pltpu.HBM) for array in inputs]
    out = pl.pallas_call(
        kernel,
        out_shape=jax.ShapeDtypeStruct((ROWS * 4, BLK), F32),
        in_specs=[smem, smem, vmem, pl.BlockSpec(memory_space=pltpu.HBM)],
        out_specs=vmem,
        scratch_shapes=[
            pltpu.VMEM((2, NAUX * O, BLK), F32),
            pltpu.VMEM((ROWS, NAUX), BF16),
            pltpu.VMEM((ROWS, NAUX), BF16),
            pltpu.VMEM((PAIR, PACK), F32),
            pltpu.VMEM((PAIR, NAUX), BF16),
            pltpu.VMEM((PAIR, NAUX), BF16),
            pltpu.VMEM((PAIR, NAUX), F32),
            pltpu.VMEM((PAIR, PACK), F32),
            pltpu.VMEM((5, PAIR, PACK), F32),
            pltpu.VMEM((2, 7, HALF, PACK), F32),
            pltpu.VMEM((2, TILE, NAUX), BF16),
            pltpu.VMEM((2, TILE, NAUX), BF16),
            pltpu.SMEM((O * 2 * NPB * 3,), F32),
            pltpu.SMEM((4 * NPB * 3,), F32),
            dma((NPB, 2)), dma((3, CHUNKS, 2)), dma((3, CHUNKS)),
            dma((2, 7)), dma((2, 7)), dma((2, 7)), dma((2, 8)),
            dma((2, RING + EARLY)), dma((2, RING + EARLY)), dma((2, RING)), dma((2, RING)), dma((2, RING)), dma((2, RING)), dma((2, RING)), dma((2, RING)),
        ],
        compiler_params=pltpu.CompilerParams(collective_id=0, has_side_effects=True, vmem_limit_bytes=VMEM_LIMIT),
        name="amplitudes",
    )(*inputs)
    return (out * SCALE).reshape(O, TILE, 2, 2, BLK).transpose(0, 1, 3, 2, 4).reshape(O, TILE, 2, TILE)


def solution(mesh):
    placed = (P(None, None, "va"), P(), P(), P())
    return jax.shard_map(
        body, mesh=mesh, in_specs=placed, out_specs=P(None, "va", "aux", "vb"), check_vma=False
    )
```
